32 devices in a mesh: tm: 4 (over x, core), space: 8 (over z, y).
Axes of the slice: x: 2, y: 2, z: 4, core: 2. Of those that a mesh axis runs over, the one named last changes fastest.
Arguments:
- video_in: bfloat16 [16, 8, 16, 3072], P('tm', 'space'), may hold values from -6 to 6
- neighbours: int32 [8, 8], replicated, may hold values from 0 to 8, as said below
- valid_frames: int32 [8], replicated, may hold values from 0 to 16, as said below
- norm1_gain: float32 [192], replicated, may hold values from 0.1 to 1.9
- conv1_weight: bfloat16 [9, 576, 192], replicated, may hold values from -0.078125 to 0.078125
- conv1_bias: float32 [192], replicated, may hold values from -3 to 3
- norm2_gain: float32 [192], replicated, may hold values from 0.1 to 1.9
- conv2_weight: bfloat16 [9, 576, 192], replicated, may hold values from -0.078125 to 0.078125
- conv2_bias: float32 [192], replicated, may hold values from -3 to 3
Outputs:
- block_out: bfloat16 [16, 8, 16, 3072], P('tm', 'space')
The draws below stay inside these ranges and needn't reach their ends.
Inputs may be any that keep to these rules, and one draw needn't show every extreme that they name: `neighbours`: entry k of a tile's row names the tile beside it in direction k of one placement of all tiles on a grid of 1 row by 8 columns, directions ordered (row, column) = (-1,-1), (-1,0), (-1,1), (0,-1), (0,1), (1,-1), (1,0), (1,1); 8 where that place lies outside the grid. `valid_frames`: frames from this number on are padding in that tile's track.
All inputs are finite; a program needn't handle non-finite values.
Results may differ from the reference program's by a relative error of at most 0.0037.
Values may be sent and summed in bfloat16 or wider, within the bound.
No kernel may reach another device: no remote copies, remote signals or barrier semaphores. Data moves between devices by JAX's collectives and lax.ppermute only.
A program may use at most 64 MiB of HBM per device.

```python
import jax
import jax.numpy as jnp
from jax import lax

C = 192
TS = 16
GRID_W = 8
TILES = 8
GH = 1
F = 16


def tile_layout(key):
    row_key = jax.random.fold_in(key, 101)
    col_key = jax.random.fold_in(key, 102)
    row_order = jax.random.permutation(row_key, GH)

    def shuffled(subkey):
        return jax.random.permutation(subkey, GRID_W)
    col_order = jax.vmap(shuffled)(jax.random.split(col_key, GH))
    grid_row = jnp.repeat(row_order, GRID_W).astype(jnp.int32)
    grid_col = col_order.reshape(-1).astype(jnp.int32)
    return (grid_row, grid_col)


def draw_neighbours(key, part):
    grid_row, grid_col = tile_layout(key)
    placed = jnp.zeros((TILES,), jnp.int32).at[grid_row * GRID_W + grid_col].set(jnp.arange(TILES, dtype=jnp.int32))
    columns = []
    for row_step in (-1, 0, 1):
        for col_step in (-1, 0, 1):
            if row_step == 0 and col_step == 0:
                continue
            near_row = grid_row + row_step
            near_col = grid_col + col_step
            inside = (near_row >= 0) & (near_row < GH) & (near_col >= 0) & (near_col < GRID_W)
            target = placed[jnp.clip(near_row, 0, GH - 1) * GRID_W + jnp.clip(near_col, 0, GRID_W - 1)]
            columns.append(jnp.where(inside, target, TILES))
    return jnp.stack(columns, axis=1).astype(jnp.int32)


def draw_valid_frames(key, part):
    grid_row = tile_layout(key)[0]
    cut_key = jax.random.fold_in(key, 103)
    top_cut = jax.random.randint(jax.random.fold_in(cut_key, 1), (), 0, GH // 4 + 1)
    bottom_cut = jax.random.randint(jax.random.fold_in(cut_key, 2), (), 0, GH // 4 + 1)
    in_band = (grid_row >= top_cut) & (grid_row < GH - bottom_cut)
    lengths = jax.random.randint(jax.random.fold_in(key, 104), (TILES,), 1, F + 1)
    whole_track = jax.random.randint(jax.random.fold_in(key, 105), (TILES,), 0, 2) == 1
    frame_counts = jnp.where(whole_track, F, lengths)
    return jnp.where(in_band, frame_counts, 0).astype(jnp.int32)


def block_scale(stream_key, dims, cuts, smallest, high):
    def one(position, shards_of):
        steps = jax.random.uniform(jax.random.fold_in(jax.random.fold_in(stream_key, 6), position), (shards_of,), jnp.float32, smallest / len(cuts), high / len(cuts))
        return jnp.repeat(jnp.exp(steps), dims[position] // shards_of).reshape((-1,) + (1,) * (len(dims) - position - 1))

    loudness = one(*cuts[0])
    for cut in cuts[1:]:
        loudness = loudness * one(*cut)
    return loudness


def centred(key, extent, deviation, most, cuts=(), kind=jnp.bfloat16):
    entries = deviation * jax.random.normal(key, extent, jnp.float32)
    if cuts:
        entries = entries * block_scale(key, extent, cuts, -0.22, 0.18)
    return jnp.clip(entries, -most, most).astype(kind)


def setup_inputs(seed: int = 0) -> dict:
    arg_keys = jax.random.split(jax.random.key(seed), 10)
    video_in = centred(arg_keys[0], (F, TILES, TS, TS * C), 1.0, 6.0, ((0, 4), (1, 8)))
    neighbours = draw_neighbours(jax.random.fold_in(arg_keys[9], 71), 0)
    valid_frames = draw_valid_frames(jax.random.fold_in(arg_keys[9], 71), 0)
    norm1_gain = jnp.clip(1.0 + 0.18 * jax.random.normal(arg_keys[3], (C,), jnp.float32), 0.1, 1.9)
    conv1_weight = centred(arg_keys[4], (9, 3 * C, C), (27 * C) ** -0.5, 0.078125)
    conv1_bias = centred(arg_keys[5], (C,), 0.5, 3.0, (), jnp.float32)
    norm2_gain = jnp.clip(1.0 + 0.18 * jax.random.normal(arg_keys[6], (C,), jnp.float32), 0.1, 1.9)
    conv2_weight = centred(arg_keys[7], (9, 3 * C, C), (27 * C) ** -0.5, 0.078125)
    conv2_bias = centred(arg_keys[8], (C,), 0.5, 3.0, (), jnp.float32)
    return dict(video_in=video_in, neighbours=neighbours, valid_frames=valid_frames, norm1_gain=norm1_gain, conv1_weight=conv1_weight, conv1_bias=conv1_bias, norm2_gain=norm2_gain, conv2_weight=conv2_weight, conv2_bias=conv2_bias)


epsilon = 1e-06

def norm_silu(values, scale_gain):
    square = lax.optimization_barrier(jnp.mean(values * values, axis=-1, keepdims=True))
    return jax.nn.silu(values * lax.rsqrt(square + epsilon) * scale_gain)

def conv_tile(framed, weight):
    frames_out = framed.shape[0] - 2
    side_len = framed.shape[1] - 2
    channels = framed.shape[-1]
    widened = jnp.concatenate([framed[:, :, col_off:col_off + side_len] for col_off in range(3)], axis=-1)
    summed = jnp.zeros((frames_out * side_len * side_len, channels), jnp.float32)
    for time_off in range(3):
        for row_off in range(3):
            window = widened[time_off:time_off + frames_out, row_off:row_off + side_len].reshape(-1, 3 * channels)
            summed = summed + jnp.dot(window, weight[time_off * 3 + row_off], preferred_element_type=jnp.float32)
    return summed.reshape(frames_out, side_len, side_len, channels)

def extend_tile(activation, tile_index, neighbours):
    nearby = lax.dynamic_index_in_dim(neighbours, tile_index, 0, keepdims=False)

    def fetch_tile(direction):
        other_tile = nearby[direction]
        fetched = lax.dynamic_index_in_dim(activation, jnp.minimum(other_tile, TILES - 1).astype(jnp.int32), 1, keepdims=False)
        return fetched * (other_tile < TILES).astype(activation.dtype)
    centre = lax.dynamic_index_in_dim(activation, tile_index, 1, keepdims=False)
    top_row = jnp.concatenate([fetch_tile(0)[:, -1:, -1:], fetch_tile(1)[:, -1:, :], fetch_tile(2)[:, -1:, :1]], axis=2)
    middle = jnp.concatenate([fetch_tile(3)[:, :, -1:], centre, fetch_tile(4)[:, :, :1]], axis=2)
    bottom_row = jnp.concatenate([fetch_tile(5)[:, :1, -1:], fetch_tile(6)[:, :1, :], fetch_tile(7)[:, :1, :1]], axis=2)
    framed = jnp.concatenate([top_row, middle, bottom_row], axis=1)
    return jnp.pad(framed, ((2, 0), (0, 0), (0, 0), (0, 0)))

def reference(video_in, neighbours, valid_frames, norm1_gain, conv1_weight, conv1_bias, norm2_gain, conv2_weight, conv2_bias):
    voxels = video_in.reshape(F, TILES, TS, TS, C)
    frame_ids = jnp.arange(F, dtype=jnp.int32)
    present = frame_ids[:, None] < valid_frames[None, :]
    masked = voxels * present[:, :, None, None, None].astype(voxels.dtype)
    activation = norm_silu(masked.astype(jnp.float32), norm1_gain).astype(jnp.bfloat16)
    tile_range = jnp.arange(TILES, dtype=jnp.int32)

    def frame_weights(tile_index):
        return lax.dynamic_index_in_dim(present, tile_index, 1, keepdims=False).astype(jnp.float32)[:, None, None, None]

    def first_pass(tile_index):
        summed = conv_tile(extend_tile(activation, tile_index, neighbours), conv1_weight)
        return norm_silu((summed + conv1_bias) * frame_weights(tile_index), norm2_gain).astype(jnp.bfloat16)
    hidden = jnp.moveaxis(lax.map(first_pass, tile_range), 0, 1)

    def second_pass(tile_index):
        summed = conv_tile(extend_tile(hidden, tile_index, neighbours), conv2_weight)
        residual = lax.dynamic_index_in_dim(masked, tile_index, 1, keepdims=False).astype(jnp.float32)
        return ((summed + conv2_bias) * frame_weights(tile_index) + residual).astype(jnp.bfloat16)
    block_out = jnp.moveaxis(lax.map(second_pass, tile_range), 0, 1)
    return block_out.reshape(F, TILES, TS, TS * C)
```

```python
import functools
from functools import partial

import jax
import jax.numpy as jnp
from jax import lax
from jax.experimental import pallas as pl
from jax.experimental.pallas import tpu as pltpu
from jax.sharding import PartitionSpec as P

epsilon = 1e-06


def shifted(value, axis, steps):
    count = lax.axis_size(axis)
    first, last = (max(0, -steps), min(count, count - steps))
    return lax.ppermute(value, axis, [(source, source + steps) for source in range(first, last)])


def norm_silu(values, scale_gain):
    square = jnp.mean(values * values, axis=-1, keepdims=True)
    return jax.nn.silu(values * lax.rsqrt(square + epsilon) * scale_gain)


def conv_tile(framed, weight):
    frames_out = framed.shape[0] - 2
    side_len = framed.shape[1] - 2
    channels = framed.shape[-1]
    widened = jnp.concatenate(
        [framed[:, :, col_off : col_off + side_len] for col_off in range(3)], axis=-1
    )
    summed = jnp.zeros((frames_out * side_len * side_len, channels), jnp.float32)
    for time_off in range(3):
        for row_off in range(3):
            window = widened[
                time_off : time_off + frames_out, row_off : row_off + side_len
            ].reshape(-1, 3 * channels)
            summed = summed + jnp.dot(
                window, weight[time_off * 3 + row_off], preferred_element_type=jnp.float32
            )
    return summed.reshape(frames_out, side_len, side_len, channels)


def edge_pack(activation):
    return jnp.stack(
        [
            activation[:, :, -1],
            activation[:, :, :, -1],
            activation[:, :, :, 0],
            activation[:, :, 0],
        ],
        axis=2,
    )


def fold_edges(totals, portion, offset, nearby):
    amount = portion.shape[1]
    tile_ids = jnp.arange(amount, dtype=jnp.int32)
    choose = (nearby[:, :, None] == tile_ids[None, None, :]).astype(jnp.bfloat16)
    side_choose = jnp.stack([choose[:, 1], choose[:, 3], choose[:, 4], choose[:, 6]], axis=1)
    corner_choose = jnp.stack([choose[:, 0], choose[:, 2], choose[:, 5], choose[:, 7]], axis=1)
    corner_source = jnp.stack(
        [portion[:, :, 0, -1], portion[:, :, 0, 0], portion[:, :, 3, -1], portion[:, :, 3, 0]],
        axis=2,
    )
    new_sides = jnp.einsum(
        "djn,fnjxc->fdjxc", side_choose, portion, preferred_element_type=jnp.float32
    )
    new_corners = jnp.einsum(
        "djn,fnjc->fdjc", corner_choose, corner_source, preferred_element_type=jnp.float32
    )
    return (new_sides.astype(jnp.bfloat16), new_corners.astype(jnp.bfloat16))


def empty_rims(frame_count, activation):
    tiles_dev, side_len, channels = (activation.shape[1], activation.shape[2], activation.shape[4])
    return (
        jnp.zeros((frame_count, tiles_dev, 4, side_len, channels), jnp.bfloat16),
        jnp.zeros((frame_count, tiles_dev, 4, channels), jnp.bfloat16),
    )


def assemble(longer, side_rims, corners):
    top_row = jnp.concatenate([corners[:, :, 0:1], side_rims[:, :, 0], corners[:, :, 1:2]], axis=2)
    bottom_row = jnp.concatenate(
        [corners[:, :, 2:3], side_rims[:, :, 3], corners[:, :, 3:4]], axis=2
    )
    middle = jnp.concatenate(
        [side_rims[:, :, 1][:, :, :, None], longer, side_rims[:, :, 2][:, :, :, None]], axis=3
    )
    return jnp.concatenate([top_row[:, :, None], middle, bottom_row[:, :, None]], axis=2)


def extend(activation, nearby):
    frames_dev = activation.shape[0]
    folder = partial(fold_edges, nearby=nearby)
    side_rims, corners = folder(
        empty_rims(frames_dev, activation),
        lax.all_gather(edge_pack(activation), "space", axis=1, tiled=True),
        jnp.int32(0),
    )
    prev_act, prev_sides, prev_corners = shifted(
        (activation[frames_dev - 2 :], side_rims[frames_dev - 2 :], corners[frames_dev - 2 :]),
        "tm",
        1,
    )
    longer = jnp.concatenate([prev_act, activation], axis=0)
    side_rims = jnp.concatenate([prev_sides, side_rims], axis=0)
    corners = jnp.concatenate([prev_corners, corners], axis=0)
    return assemble(longer, side_rims, corners)


def blank_tile(pieces, tile_valid):
    framed = pieces[0]
    return jnp.zeros(
        (framed.shape[0] - 2, framed.shape[1] - 2, framed.shape[2] - 2, framed.shape[3]),
        jnp.bfloat16,
    )


def home_tiles(inputs, home_valid, first_frame, worker):
    pieces = tuple((stacked[:, 0] for stacked in inputs))
    results = [lax.cond(home_valid[0] > first_frame, worker, blank_tile, pieces, home_valid[0])]
    return jnp.stack(results, axis=1)


def general_path(
    video_in,
    neighbours,
    valid_frames,
    norm1_gain,
    conv1_weight,
    conv1_bias,
    norm2_gain,
    conv2_weight,
    conv2_bias,
):
    frames_dev, tiles_dev, side_len, merged = video_in.shape
    channels = norm1_gain.shape[0]
    voxels = video_in.reshape(frames_dev, tiles_dev, side_len, side_len, channels)
    first_frame = lax.axis_index("tm") * frames_dev
    home_ids = lax.axis_index("space") * tiles_dev + jnp.arange(tiles_dev, dtype=jnp.int32)
    home_valid = jnp.take(valid_frames, home_ids)
    nearby = jnp.take(neighbours, home_ids, axis=0)
    frame_pos = first_frame + jnp.arange(frames_dev, dtype=jnp.int32)
    present = (frame_pos[:, None] < home_valid[None, :]).astype(jnp.bfloat16)
    masked = voxels * present[:, :, None, None, None]
    activation = norm_silu(masked.astype(jnp.float32), norm1_gain).astype(jnp.bfloat16)

    def frame_weights(tile_valid):
        return (frame_pos < tile_valid).astype(jnp.float32)[:, None, None, None]

    def first_worker(pieces, tile_valid):
        summed = conv_tile(pieces[0], conv1_weight)
        return norm_silu((summed + conv1_bias) * frame_weights(tile_valid), norm2_gain).astype(
            jnp.bfloat16
        )

    def second_worker(pieces, tile_valid):
        summed = conv_tile(pieces[0], conv2_weight)
        return (
            (summed + conv2_bias) * frame_weights(tile_valid) + pieces[1].astype(jnp.float32)
        ).astype(jnp.bfloat16)

    padded = extend(activation, nearby)
    hidden = home_tiles((padded,), home_valid, first_frame, first_worker)
    padded = extend(hidden, nearby)
    block_out = home_tiles((padded, masked), home_valid, first_frame, second_worker)
    return block_out.reshape(frames_dev, tiles_dev, side_len, side_len * channels)


def silu(a):
    return a*(0.5+0.5*jnp.tanh(0.5*a))
def normsilu(v,g):
    ss=jnp.mean(v*v,axis=-1,keepdims=True)
    return silu(v*lax.rsqrt(ss+epsilon)*g)
LANE=256
def put(B,idx,h,C):
    S=h.shape[0]
    row=lax.broadcasted_iota(jnp.int32,h.shape,0)
    down=jnp.where(row==0,0.0,pltpu.roll(h,1,0))
    up=jnp.where(row==S-1,0.0,pltpu.roll(h,S-1,0))
    B[idx+(slice(None),slice(0,C))]=down.astype(jnp.bfloat16)
    B[idx+(slice(None),slice(LANE,LANE+C))]=h.astype(jnp.bfloat16)
    B[idx+(slice(None),slice(2*LANE,2*LANE+C))]=up.astype(jnp.bfloat16)
def zero_pads(B,C):
    X,Fr,S,L=B.shape
    z=jnp.zeros((Fr,S,LANE-C),B.dtype)
    def body(x,_):
        for q in range(3):
            B[x,:,:,q*LANE+C:(q+1)*LANE]=z
        return 0
    lax.fori_loop(0,X,body,0)
def conv(B,x0,G,nf,w,C):
    S=B.shape[2]
    acc=None
    for p in range(3):
        for r in range(3):
            lhs=B[pl.ds(x0+r,G),p:p+nf].reshape(G*nf*S,3*LANE)
            d=jnp.dot(lhs,w[p*3+r],preferred_element_type=jnp.float32)
            acc=d if acc is None else acc+d
    return acc.reshape(G,nf,S,C)
def spread_weights(wt,w,C):
    z=jnp.zeros((LANE-C,C),w.dtype)
    def body(p,_):
        for q in range(3):
            t=wt[3*p+q].T
            for r in range(3):
                w[p*3+r,q*LANE:q*LANE+C]=t[r*C:(r+1)*C]
                w[p*3+r,q*LANE+C:(q+1)*LANE]=z
        return 0
    lax.fori_loop(0,3,body,0)
def whole(nb,vf,own,prev,rim,prim,g1,w1h,b1,g2,w2h,b2,out,B1,B2,w1,w2,wt1,wt2,sem1,sem2,*,G1,G2):
    Fd,S,M=own.shape; C=g1.shape[0]; X=M//C
    c1=pltpu.make_async_copy(w1h,wt1,sem1.at[0]); c2=pltpu.make_async_copy(w2h,wt2,sem2.at[0])
    c1.start(); c2.start()
    first=lax.axis_index("tm")*Fd; vs,vl,vr=tracks(nb,vf)
    zero_pads(B1,C); zero_pads(B2,C)
    gv1=g1[...].reshape(1,C); gv2=g2[...].reshape(1,C); bv1=b1[...].reshape(1,C); bv2=b2[...].reshape(1,C)
    def there(f,v):
        return ((f>=0)&(f<v)).astype(jnp.float32)
    def act(pair,f,v,x,fi):
        m=there(f,v)
        vv=pair.astype(jnp.float32)*m
        for j in range(2):
            put(B1,(x+j,fi),normsilu(vv[:,j*C:(j+1)*C],gv1),C)
    for f in range(Fd):
        act(prim[0,f],first-Fd+f,vl,0,f); act(rim[0,f],first+f,vl,0,Fd+f)
        act(prim[1,f],first-Fd+f,vr,X+2,f); act(rim[1,f],first+f,vr,X+2,Fd+f)
    def actloop(k,_):
        ds=pl.ds(pl.multiple_of(k*2*C,128),2*C)
        for f in range(Fd):
            act(prev[f,:,ds],first-Fd+f,vs,2+2*k,f)
            act(own[f,:,ds],first+f,vs,2+2*k,Fd+f)
        return 0
    lax.fori_loop(0,X//2,actloop,0)
    c1.wait(); spread_weights(wt1,w1,C)
    nf1=Fd+2
    def c1loop(i,_):
        x0=i*G1
        a=conv(B1,x0,G1,nf1,w1,C)
        for g in range(G1):
            x=x0+g-1
            v=jnp.where(x<0,vl,jnp.where(x>=X,vr,vs))
            for f in range(nf1):
                m=there(first-2+f,v)
                put(B2,(x0+g,f),normsilu((a[g,f]+bv1)*m,gv2),C)
        return 0
    lax.fori_loop(0,(X+2)//G1,c1loop,0)
    c2.wait(); spread_weights(wt2,w2,C)
    def c2loop(i,_):
        x0=i*G2
        a=conv(B2,x0,G2,Fd,w2,C)
        for f in range(Fd):
            m=there(first+f,vs)
            for g in range(0,G2,2):
                ds=pl.ds(pl.multiple_of((x0+g)*C,128),2*C)
                res=own[f,:,ds].astype(jnp.float32)*m
                o=jnp.concatenate([(a[g,f]+bv2)*m,(a[g+1,f]+bv2)*m],-1)+res
                out[f,:,ds]=o.astype(jnp.bfloat16)
        return 0
    lax.fori_loop(0,X//G2,c2loop,0)
def call_whole(nb,vf,own,prev,rim,prim,g1,w1,b1,g2,w2,b2,G1=6,G2=8):
    Fd,S,M=own.shape; C=g1.shape[0]; X=M//C
    V=pl.BlockSpec(memory_space=pltpu.VMEM); A=pl.BlockSpec(memory_space=pl.ANY); SM=pl.BlockSpec(memory_space=pltpu.SMEM)
    return pl.pallas_call(functools.partial(whole,G1=G1,G2=G2),
        out_shape=jax.ShapeDtypeStruct(own.shape,own.dtype),
        in_specs=[SM,SM,V,V,V,V,V,A,V,V,A,V],out_specs=V,
        scratch_shapes=[pltpu.VMEM((X+4,2*Fd,S,3*LANE),jnp.bfloat16),pltpu.VMEM((X+2,Fd+2,S,3*LANE),jnp.bfloat16),
            pltpu.VMEM((9,3*LANE,C),jnp.bfloat16),pltpu.VMEM((9,3*LANE,C),jnp.bfloat16),pltpu.VMEM((9,C,3*C),jnp.bfloat16),pltpu.VMEM((9,C,3*C),jnp.bfloat16),pltpu.SemaphoreType.DMA((1,)),pltpu.SemaphoreType.DMA((1,))],
        compiler_params=pltpu.CompilerParams(vmem_limit_bytes=60*2**20),
    )(nb,vf,own,prev,rim,prim,g1,jnp.swapaxes(w1,1,2),b1,g2,jnp.swapaxes(w2,1,2),b2)


LEFT, RIGHT = 3, 4


def tracks(nb, vf):
    me = lax.axis_index("space")
    tiles = nb.shape[0]

    def of(tile):
        return jnp.where(tile < tiles, vf[jnp.minimum(tile, tiles - 1)], 0)

    return vf[me], of(nb[me, LEFT]), of(nb[me, RIGHT])


def pick_kernel(nb, mine, pair, *outs):
    tiles = nb.shape[0]
    me = lax.axis_index("space")
    for step, out in enumerate(outs):
        there = lax.rem(me + 2 * (step + 1), tiles)
        for side, column in ((0, LEFT), (1, RIGHT)):
            source = nb[there, column]

            @pl.when(source == me)
            def _():
                out[side] = mine[1 - side]

            @pl.when(source != me)
            def _():
                out[side] = pair[1 - side]


def rims_kernel(nb, mine, pair, *rest):
    received, out = rest[:-1], rest[-1]
    tiles = nb.shape[0]
    half = tiles // 2
    me = lax.axis_index("space")
    for side, column in ((0, LEFT), (1, RIGHT)):
        source = nb[me, column]
        step = lax.rem(me // 2 - source // 2 + tiles, half)
        at_home = (step == 0) | (source >= tiles)

        @pl.when(at_home & (source == me ^ 1))
        def _():
            out[side] = pair[1 - side]

        @pl.when(at_home & (source != me ^ 1))
        def _():
            out[side] = mine[1 - side]

        for s, arrived in enumerate(received):

            @pl.when((step == s + 1) & (source < tiles))
            def _():
                out[side] = arrived[side]


def exchange(own, neighbours, channels):
    count = lax.axis_size("space")
    vmem = pl.BlockSpec(memory_space=pltpu.VMEM)
    smem = pl.BlockSpec(memory_space=pltpu.SMEM)
    mine = jnp.stack([own[:, :, : 2 * channels], own[:, :, -2 * channels :]])
    pair = lax.ppermute(mine, "space", [(i, i ^ 1) for i in range(count)])
    piece = jax.ShapeDtypeStruct(mine.shape, mine.dtype)
    steps = count // 2 - 1
    sent = pl.pallas_call(
        pick_kernel,
        out_shape=[piece] * steps,
        in_specs=[smem, vmem, vmem],
        out_specs=[vmem] * steps,
    )(neighbours, mine, pair)
    received = [
        lax.ppermute(value, "space", [(i, (i + 2 * (s + 1)) % count) for i in range(count)])
        for s, value in enumerate(sent)
    ]
    return pl.pallas_call(
        rims_kernel,
        out_shape=piece,
        in_specs=[smem] + [vmem] * (2 + steps),
        out_specs=vmem,
    )(neighbours, mine, pair, *received)


def row_path(video_in, neighbours, valid_frames, gain1, weight1, bias1, gain2, weight2, bias2):
    own = video_in[:, 0]
    prev = shifted(own, "tm", 1)
    rim = exchange(own, neighbours, gain1.shape[0])
    prev_rim = shifted(rim, "tm", 1)
    out = call_whole(neighbours, valid_frames, own, prev, rim, prev_rim, gain1, weight1, bias1, gain2, weight2, bias2)
    return out[:, None]


def on_device(video_in, neighbours, *rest):
    frames_dev, tiles_dev = video_in.shape[:2]
    tiles = neighbours.shape[0]
    if tiles_dev != 1 or tiles % 2 or frames_dev < 4:
        return general_path(video_in, neighbours, *rest)
    beyond = jnp.concatenate([neighbours[:, :LEFT], neighbours[:, RIGHT + 1 :]], axis=1)
    return lax.cond(jnp.any(beyond < tiles), general_path, row_path, video_in, neighbours, *rest)


def solution(mesh):
    in_specs = (P("tm", "space", None, None), P(), P(), P(), P(), P(), P(), P(), P())
    out_specs = P("tm", "space", None, None)
    return jax.shard_map(
        on_device, mesh=mesh, in_specs=in_specs, out_specs=out_specs, check_vma=False
    )
```

```python
import functools
from functools import partial

import jax
import jax.numpy as jnp
from jax import lax
from jax.experimental import pallas as pl
from jax.experimental.pallas import tpu as pltpu
from jax.sharding import PartitionSpec as P

epsilon = 1e-06


def shifted(value, axis, steps):
    count = lax.axis_size(axis)
    first, last = (max(0, -steps), min(count, count - steps))
    return lax.ppermute(value, axis, [(source, source + steps) for source in range(first, last)])


def norm_silu(values, scale_gain):
    square = jnp.mean(values * values, axis=-1, keepdims=True)
    return jax.nn.silu(values * lax.rsqrt(square + epsilon) * scale_gain)


def conv_tile(framed, weight):
    frames_out = framed.shape[0] - 2
    side_len = framed.shape[1] - 2
    channels = framed.shape[-1]
    widened = jnp.concatenate(
        [framed[:, :, col_off : col_off + side_len] for col_off in range(3)], axis=-1
    )
    summed = jnp.zeros((frames_out * side_len * side_len, channels), jnp.float32)
    for time_off in range(3):
        for row_off in range(3):
            window = widened[
                time_off : time_off + frames_out, row_off : row_off + side_len
            ].reshape(-1, 3 * channels)
            summed = summed + jnp.dot(
                window, weight[time_off * 3 + row_off], preferred_element_type=jnp.float32
            )
    return summed.reshape(frames_out, side_len, side_len, channels)


def edge_pack(activation):
    return jnp.stack(
        [
            activation[:, :, -1],
            activation[:, :, :, -1],
            activation[:, :, :, 0],
            activation[:, :, 0],
        ],
        axis=2,
    )


def fold_edges(totals, portion, offset, nearby):
    amount = portion.shape[1]
    tile_ids = jnp.arange(amount, dtype=jnp.int32)
    choose = (nearby[:, :, None] == tile_ids[None, None, :]).astype(jnp.bfloat16)
    side_choose = jnp.stack([choose[:, 1], choose[:, 3], choose[:, 4], choose[:, 6]], axis=1)
    corner_choose = jnp.stack([choose[:, 0], choose[:, 2], choose[:, 5], choose[:, 7]], axis=1)
    corner_source = jnp.stack(
        [portion[:, :, 0, -1], portion[:, :, 0, 0], portion[:, :, 3, -1], portion[:, :, 3, 0]],
        axis=2,
    )
    new_sides = jnp.einsum(
        "djn,fnjxc->fdjxc", side_choose, portion, preferred_element_type=jnp.float32
    )
    new_corners = jnp.einsum(
        "djn,fnjc->fdjc", corner_choose, corner_source, preferred_element_type=jnp.float32
    )
    return (new_sides.astype(jnp.bfloat16), new_corners.astype(jnp.bfloat16))


def empty_rims(frame_count, activation):
    tiles_dev, side_len, channels = (activation.shape[1], activation.shape[2], activation.shape[4])
    return (
        jnp.zeros((frame_count, tiles_dev, 4, side_len, channels), jnp.bfloat16),
        jnp.zeros((frame_count, tiles_dev, 4, channels), jnp.bfloat16),
    )


def assemble(longer, side_rims, corners):
    top_row = jnp.concatenate([corners[:, :, 0:1], side_rims[:, :, 0], corners[:, :, 1:2]], axis=2)
    bottom_row = jnp.concatenate(
        [corners[:, :, 2:3], side_rims[:, :, 3], corners[:, :, 3:4]], axis=2
    )
    middle = jnp.concatenate(
        [side_rims[:, :, 1][:, :, :, None], longer, side_rims[:, :, 2][:, :, :, None]], axis=3
    )
    return jnp.concatenate([top_row[:, :, None], middle, bottom_row[:, :, None]], axis=2)


def extend(activation, nearby):
    frames_dev = activation.shape[0]
    folder = partial(fold_edges, nearby=nearby)
    side_rims, corners = folder(
        empty_rims(frames_dev, activation),
        lax.all_gather(edge_pack(activation), "space", axis=1, tiled=True),
        jnp.int32(0),
    )
    prev_act, prev_sides, prev_corners = shifted(
        (activation[frames_dev - 2 :], side_rims[frames_dev - 2 :], corners[frames_dev - 2 :]),
        "tm",
        1,
    )
    longer = jnp.concatenate([prev_act, activation], axis=0)
    side_rims = jnp.concatenate([prev_sides, side_rims], axis=0)
    corners = jnp.concatenate([prev_corners, corners], axis=0)
    return assemble(longer, side_rims, corners)


def blank_tile(pieces, tile_valid):
    framed = pieces[0]
    return jnp.zeros(
        (framed.shape[0] - 2, framed.shape[1] - 2, framed.shape[2] - 2, framed.shape[3]),
        jnp.bfloat16,
    )


def home_tiles(inputs, home_valid, first_frame, worker):
    pieces = tuple((stacked[:, 0] for stacked in inputs))
    results = [lax.cond(home_valid[0] > first_frame, worker, blank_tile, pieces, home_valid[0])]
    return jnp.stack(results, axis=1)


def general_path(
    video_in,
    neighbours,
    valid_frames,
    norm1_gain,
    conv1_weight,
    conv1_bias,
    norm2_gain,
    conv2_weight,
    conv2_bias,
):
    frames_dev, tiles_dev, side_len, merged = video_in.shape
    channels = norm1_gain.shape[0]
    voxels = video_in.reshape(frames_dev, tiles_dev, side_len, side_len, channels)
    first_frame = lax.axis_index("tm") * frames_dev
    home_ids = lax.axis_index("space") * tiles_dev + jnp.arange(tiles_dev, dtype=jnp.int32)
    home_valid = jnp.take(valid_frames, home_ids)
    nearby = jnp.take(neighbours, home_ids, axis=0)
    frame_pos = first_frame + jnp.arange(frames_dev, dtype=jnp.int32)
    present = (frame_pos[:, None] < home_valid[None, :]).astype(jnp.bfloat16)
    masked = voxels * present[:, :, None, None, None]
    activation = norm_silu(masked.astype(jnp.float32), norm1_gain).astype(jnp.bfloat16)

    def frame_weights(tile_valid):
        return (frame_pos < tile_valid).astype(jnp.float32)[:, None, None, None]

    def first_worker(pieces, tile_valid):
        summed = conv_tile(pieces[0], conv1_weight)
        return norm_silu((summed + conv1_bias) * frame_weights(tile_valid), norm2_gain).astype(
            jnp.bfloat16
        )

    def second_worker(pieces, tile_valid):
        summed = conv_tile(pieces[0], conv2_weight)
        return (
            (summed + conv2_bias) * frame_weights(tile_valid) + pieces[1].astype(jnp.float32)
        ).astype(jnp.bfloat16)

    padded = extend(activation, nearby)
    hidden = home_tiles((padded,), home_valid, first_frame, first_worker)
    padded = extend(hidden, nearby)
    block_out = home_tiles((padded, masked), home_valid, first_frame, second_worker)
    return block_out.reshape(frames_dev, tiles_dev, side_len, side_len * channels)


LANE = 256


def silu(a):
    return a * (0.5 + 0.5 * jnp.tanh(0.5 * a))


def normed(v, gain):
    square = jnp.mean(v * v, axis=-1, keepdims=True)
    return silu(v * lax.rsqrt(square + epsilon) * gain)


def put(buf, x, f0, h):
    n, side, channels = h.shape
    row = lax.broadcasted_iota(jnp.int32, h.shape, 1)
    down = jnp.where(row == 0, 0.0, pltpu.roll(h, 1, 1))
    up = jnp.where(row == side - 1, 0.0, pltpu.roll(h, side - 1, 1))
    for q, t in enumerate((down, h, up)):
        buf[x, f0 : f0 + n, :, q * LANE : q * LANE + channels] = t.astype(jnp.bfloat16)


def zero_pads(buf, channels):
    columns, frames, side, _ = buf.shape
    zero = jnp.zeros((frames, side, LANE - channels), buf.dtype)

    def body(x, _):
        for q in range(3):
            buf[x, :, :, q * LANE + channels : (q + 1) * LANE] = zero
        return 0

    lax.fori_loop(0, columns, body, 0)


def spread(flat, weight):
    channels = weight.shape[2]
    zero = jnp.zeros((LANE - channels, channels), weight.dtype)

    def body(p, _):
        for q in range(3):
            turned = flat[3 * p + q].T
            for r in range(3):
                weight[p * 3 + r, q * LANE : q * LANE + channels] = turned[r * channels : (r + 1) * channels]
                weight[p * 3 + r, q * LANE + channels : (q + 1) * LANE] = zero
        return 0

    lax.fori_loop(0, 3, body, 0)


def conv(buf, starts, width, f0, frames, weight):
    side = buf.shape[2]
    total = None
    for p in range(3):
        for r in range(3):
            parts = [buf[pl.ds(x0 + r, width), f0 + p : f0 + p + frames] for x0 in starts]
            rows = parts[0] if len(parts) == 1 else jnp.concatenate(parts, axis=0)
            term = jnp.dot(rows.reshape(-1, 3 * LANE), weight[p * 3 + r], preferred_element_type=jnp.float32)
            total = term if total is None else total + term
    return total.reshape(len(starts) * width, frames, side, weight.shape[2])


def there(f0, frames, valid):
    frame = f0 + lax.broadcasted_iota(jnp.int32, (frames, 1, 1), 0)
    return ((frame >= 0) & (frame < valid)).astype(jnp.float32)


def act(buf, pair, f0, valid, x, at, gain):
    channels = gain.shape[1]
    values = pair.astype(jnp.float32) * there(f0, pair.shape[0], valid)
    for j in range(2):
        put(buf, x + j, at, normed(values[:, :, j * channels : (j + 1) * channels], gain))


def act_tile(buf, tile, f0, valid, at, gain):
    channels = gain.shape[1]

    def body(k, _):
        lanes = pl.ds(pl.multiple_of(k * 2 * channels, 128), 2 * channels)
        act(buf, tile[:, :, lanes], f0, valid, 2 + 2 * k, at, gain)
        return 0

    lax.fori_loop(0, tile.shape[2] // (2 * channels), body, 0)


def row_of(ref):
    return ref[...].reshape(1, -1)


def hide(total, buf, places, f0, at, bias, gain, valids):
    for g, (x, valid) in enumerate(zip(places, valids)):
        put(buf, x, at, normed((total[g] + bias) * there(f0, total.shape[1], valid), gain))


def finish(total, out, own, places, bias, f0, valid):
    channels = bias.shape[1]
    mask = there(f0, total.shape[1], valid)
    for g in range(0, len(places), 2):
        x = places[g]
        lanes = pl.ds(x * channels if isinstance(x, int) else pl.multiple_of(x * channels, 128), 2 * channels)
        both = jnp.concatenate([(total[g] + bias) * mask, (total[g + 1] + bias) * mask], axis=-1)
        out[:, :, lanes] = (both + own[:, :, lanes].astype(jnp.float32) * mask).astype(jnp.bfloat16)


def prepare_kernel(nb, vf, own, gain1, flat1, flat2, buf1, buf2, weight1, weight2, held1, held2, sem):
    first = lax.axis_index("tm") * own.shape[0]
    copy1 = pltpu.make_async_copy(flat1, held1, sem.at[0])
    copy2 = pltpu.make_async_copy(flat2, held2, sem.at[1])
    copy1.start()
    copy2.start()
    channels = gain1.shape[0]
    zero_pads(buf1, channels)
    zero_pads(buf2, channels)
    act_tile(buf1, own, first, tracks(nb, vf)[0], own.shape[0], row_of(gain1))
    copy1.wait()
    spread(held1, weight1)
    copy2.wait()
    spread(held2, weight2)


def late_kernel(nb, vf, buf1, weight1, bias1, gain2, _, buf2):
    frames = buf1.shape[1] // 2
    inner = buf2.shape[0] - 4
    f0 = lax.axis_index("tm") * frames + 2
    valid = tracks(nb, vf)[0]
    total = conv(buf1, (2,), inner, frames, frames - 2, weight1)
    hide(total, buf2, range(2, 2 + inner), f0, 4, row_of(bias1), row_of(gain2), [valid] * inner)


def early_kernel(nb, vf, prev, gain1, weight1, bias1, gain2, old1, old2, buf1, buf2):
    frames = prev.shape[0]
    inner = buf2.shape[0] - 4
    first = lax.axis_index("tm") * frames
    valid = tracks(nb, vf)[0]
    act_tile(buf1, prev, first - frames, valid, 0, row_of(gain1))
    half = inner // 2

    def body(i, _):
        x0 = 2 + i * half
        total = conv(buf1, (x0,), half, frames - 4, 4, weight1)
        hide(total, buf2, [x0 + g for g in range(half)], first - 2, 0, row_of(bias1), row_of(gain2), [valid] * half)
        return 0

    lax.fori_loop(0, 2, body, 0)


def inner_kernel(nb, vf, own, buf2, weight2, bias2, out):
    frames = own.shape[0]
    inner = buf2.shape[0] - 6
    first = lax.axis_index("tm") * frames
    valid = tracks(nb, vf)[0]
    half = inner // 2

    def body(i, _):
        x0 = 2 + i * half
        total = conv(buf2, (x0,), half, 0, frames, weight2)
        finish(total, out, own, [x0 + g for g in range(half)], row_of(bias2), first, valid)
        return 0

    lax.fori_loop(0, 2, body, 0)


def rim_kernel(nb, vf, own, rim, prev_rim, gain1, weight1, bias1, gain2, weight2, bias2, old1, old2, inner, buf1, buf2, out, staged, sem):
    frames, _, merged = own.shape
    columns = buf2.shape[0] - 2
    first = lax.axis_index("tm") * frames
    valid, left, right = tracks(nb, vf)
    for side, (x, v) in enumerate(((0, left), (columns + 2, right))):
        act(buf1, prev_rim[side], first - frames, v, x, 0, row_of(gain1))
        act(buf1, rim[side], first, v, x, frames, row_of(gain1))
    total = conv(buf1, (0, columns), 2, frames - 4, frames + 2, weight1)
    places = (0, 1, columns, columns + 1)
    hide(total, buf2, places, first - 2, 0, row_of(bias1), row_of(gain2), (left, valid, valid, right))
    total = conv(buf2, (0, columns - 2), 2, 0, frames, weight2)
    ends = (0, merged - staged.shape[3])
    for side, lane in enumerate(ends):
        lanes = pl.ds(lane, staged.shape[3])
        mask = there(first, frames, valid)
        both = jnp.concatenate([(total[2 * side + g] + row_of(bias2)) * mask for g in range(2)], axis=-1)
        staged[side] = (both + own[:, :, lanes].astype(jnp.float32) * mask).astype(jnp.bfloat16)
    copies = [pltpu.make_async_copy(staged.at[k], out.at[:, :, pl.ds(lane, staged.shape[3])], sem.at[k]) for k, lane in enumerate(ends)]
    for copy in copies:
        copy.start()
    for copy in copies:
        copy.wait()


LEFT, RIGHT = 3, 4


def tracks(nb, vf):
    me = lax.axis_index("space")
    tiles = nb.shape[0]

    def of(tile):
        return jnp.where(tile < tiles, vf[jnp.minimum(tile, tiles - 1)], 0)

    return vf[me], of(nb[me, LEFT]), of(nb[me, RIGHT])


def pick_kernel(nb, mine, pair, *outs):
    tiles = nb.shape[0]
    me = lax.axis_index("space")
    for step, out in enumerate(outs):
        there = lax.rem(me + 2 * (step + 1), tiles)
        for side, column in ((0, LEFT), (1, RIGHT)):
            source = nb[there, column]

            @pl.when(source == me)
            def _():
                out[side] = mine[1 - side]

            @pl.when(source != me)
            def _():
                out[side] = pair[1 - side]


def rims_kernel(nb, mine, pair, *rest):
    received, out = rest[:-1], rest[-1]
    tiles = nb.shape[0]
    half = tiles // 2
    me = lax.axis_index("space")
    for side, column in ((0, LEFT), (1, RIGHT)):
        source = nb[me, column]
        step = lax.rem(me // 2 - source // 2 + tiles, half)
        at_home = (step == 0) | (source >= tiles)

        @pl.when(at_home & (source == me ^ 1))
        def _():
            out[side] = pair[1 - side]

        @pl.when(at_home & (source != me ^ 1))
        def _():
            out[side] = mine[1 - side]

        for s, arrived in enumerate(received):

            @pl.when((step == s + 1) & (source < tiles))
            def _():
                out[side] = arrived[side]


def exchange(own, neighbours, channels):
    count = lax.axis_size("space")
    vmem = pl.BlockSpec(memory_space=pltpu.VMEM)
    smem = pl.BlockSpec(memory_space=pltpu.SMEM)
    mine = jnp.stack([own[:, :, : 2 * channels], own[:, :, -2 * channels :]])
    pair = lax.ppermute(mine, "space", [(i, i ^ 1) for i in range(count)])
    piece = jax.ShapeDtypeStruct(mine.shape, mine.dtype)
    steps = count // 2 - 1
    sent = pl.pallas_call(
        pick_kernel,
        out_shape=[piece] * steps,
        in_specs=[smem, vmem, vmem],
        out_specs=[vmem] * steps,
        compiler_params=pltpu.CompilerParams(vmem_limit_bytes=8 * 2**20),
    )(neighbours, mine, pair)
    received = [
        lax.ppermute(value, "space", [(i, (i + 2 * (s + 1)) % count) for i in range(count)])
        for s, value in enumerate(sent)
    ]
    return pl.pallas_call(
        rims_kernel,
        out_shape=piece,
        in_specs=[smem] + [vmem] * (2 + steps),
        out_specs=vmem,
        compiler_params=pltpu.CompilerParams(vmem_limit_bytes=8 * 2**20),
    )(neighbours, mine, pair, *received)


def call(kernel, cost, outs, ins, args, places=None, **more):
    flops, moved = cost
    return pl.pallas_call(
        kernel,
        out_shape=outs,
        in_specs=ins,
        out_specs=[VM] * len(outs) if places is None else places,
        cost_estimate=pl.CostEstimate(flops=flops, bytes_accessed=moved, transcendentals=0),
        compiler_params=pltpu.CompilerParams(vmem_limit_bytes=24 * 2**20),
        **more,
    )(*args)


VM = pl.BlockSpec(memory_space=pltpu.VMEM)
SM = pl.BlockSpec(memory_space=pltpu.SMEM)
HB = pl.BlockSpec(memory_space=pl.ANY)


def row_path(video_in, neighbours, valid_frames, gain1, weight1, bias1, gain2, weight2, bias2):
    own = video_in[:, 0]
    frames, side, merged = own.shape
    channels = gain1.shape[0]
    columns = merged // channels
    tables = (neighbours, valid_frames)
    prev = shifted(own, "tm", 1)
    rim = exchange(own, neighbours, channels)
    prev_rim = shifted(rim, "tm", 1)
    one = 2 * 27 * channels * channels * side
    space1 = pltpu.VMEM((columns + 4, 2 * frames, side, 3 * LANE), jnp.bfloat16)
    space2 = pltpu.VMEM((columns + 2, frames + 2, side, 3 * LANE), jnp.bfloat16)
    spaced = pltpu.VMEM((9, 3 * LANE, channels), jnp.bfloat16)
    flat = pltpu.VMEM((9, channels, 3 * channels), jnp.bfloat16)
    buf1, buf2, wide1, wide2 = call(
        prepare_kernel,
        (one, 4 * weight1.size),
        [space1, space2, spaced, spaced],
        [SM, SM, VM, VM, HB, HB],
        (*tables, own, gain1, jnp.swapaxes(weight1, 1, 2), jnp.swapaxes(weight2, 1, 2)),
        scratch_shapes=[flat, flat, pltpu.SemaphoreType.DMA((2,))],
    )
    (buf2,) = call(
        late_kernel,
        (one * 2 * columns, own.size),
        [space2],
        [SM, SM, VM, VM, VM, VM, VM],
        (*tables, buf1, wide1, bias1, gain2, buf2),
        input_output_aliases={6: 0},
    )
    buf1, buf2 = call(
        early_kernel,
        (one * 4 * columns, own.size),
        [space1, space2],
        [SM, SM, VM, VM, VM, VM, VM, VM, VM],
        (*tables, prev, gain1, wide1, bias1, gain2, buf1, buf2),
        input_output_aliases={7: 0, 8: 1},
    )
    (inner,) = call(
        inner_kernel,
        (one * 4 * columns, own.size),
        [jax.ShapeDtypeStruct(own.shape, own.dtype)],
        [SM, SM, VM, VM, VM, VM],
        (*tables, own, buf2, wide2, bias2),
    )
    return own, rim, prev_rim, wide1, wide2, buf1, buf2, inner


def row_end(state, tables, gain1, bias1, gain2, bias2):
    own, rim, prev_rim, wide1, wide2, buf1, buf2, inner = state
    space1, space2 = pltpu.VMEM(buf1.shape, buf1.dtype), pltpu.VMEM(buf2.shape, buf2.dtype)
    _, _, out = call(
        rim_kernel,
        (own.size * 1000, own.size),
        [space1, space2, jax.ShapeDtypeStruct(own.shape, own.dtype)],
        [SM, SM] + [VM] * 11 + [HB],
        (*tables, own, rim, prev_rim, gain1, wide1, bias1, gain2, wide2, bias2, buf1, buf2, inner),
        places=[VM, VM, HB],
        input_output_aliases={11: 0, 12: 1, 13: 2},
        scratch_shapes=[pltpu.VMEM(rim.shape, rim.dtype), pltpu.SemaphoreType.DMA((2,))],
    )
    return out[:, None]


def on_device(*args):
    video_in, neighbours, valid_frames, gain1, weight1, bias1, gain2, weight2, bias2 = args
    frames_dev, tiles_dev = video_in.shape[:2]
    tiles = neighbours.shape[0]
    if tiles_dev != 1 or tiles % 2 or frames_dev != 4:
        return general_path(*args)
    state = row_path(*args)
    beyond = jnp.concatenate([neighbours[:, :LEFT], neighbours[:, RIGHT + 1 :]], axis=1)
    return lax.cond(
        jnp.any(beyond < tiles),
        lambda state, args: general_path(*args),
        lambda state, args: row_end(state, args[1:3], gain1, bias1, gain2, bias2),
        state,
        args,
    )


def solution(mesh):
    in_specs = (P("tm", "space", None, None), P(), P(), P(), P(), P(), P(), P(), P())
    out_specs = P("tm", "space", None, None)
    return jax.shard_map(
        on_device, mesh=mesh, in_specs=in_specs, out_specs=out_specs, check_vma=False
    )
```

```python
import functools
from functools import partial

import jax
import jax.numpy as jnp
from jax import lax
from jax.experimental import pallas as pl
from jax.experimental.pallas import tpu as pltpu
from jax.sharding import PartitionSpec as P

epsilon = 1e-06


def shifted(value, axis, steps):
    count = lax.axis_size(axis)
    first, last = (max(0, -steps), min(count, count - steps))
    return lax.ppermute(value, axis, [(source, source + steps) for source in range(first, last)])


def norm_silu(values, scale_gain):
    square = jnp.mean(values * values, axis=-1, keepdims=True)
    return jax.nn.silu(values * lax.rsqrt(square + epsilon) * scale_gain)


def conv_tile(framed, weight):
    frames_out = framed.shape[0] - 2
    side_len = framed.shape[1] - 2
    channels = framed.shape[-1]
    widened = jnp.concatenate(
        [framed[:, :, col_off : col_off + side_len] for col_off in range(3)], axis=-1
    )
    summed = jnp.zeros((frames_out * side_len * side_len, channels), jnp.float32)
    for time_off in range(3):
        for row_off in range(3):
            window = widened[
                time_off : time_off + frames_out, row_off : row_off + side_len
            ].reshape(-1, 3 * channels)
            summed = summed + jnp.dot(
                window, weight[time_off * 3 + row_off], preferred_element_type=jnp.float32
            )
    return summed.reshape(frames_out, side_len, side_len, channels)


def edge_pack(activation):
    return jnp.stack(
        [
            activation[:, :, -1],
            activation[:, :, :, -1],
            activation[:, :, :, 0],
            activation[:, :, 0],
        ],
        axis=2,
    )


def fold_edges(totals, portion, offset, nearby):
    amount = portion.shape[1]
    tile_ids = jnp.arange(amount, dtype=jnp.int32)
    choose = (nearby[:, :, None] == tile_ids[None, None, :]).astype(jnp.bfloat16)
    side_choose = jnp.stack([choose[:, 1], choose[:, 3], choose[:, 4], choose[:, 6]], axis=1)
    corner_choose = jnp.stack([choose[:, 0], choose[:, 2], choose[:, 5], choose[:, 7]], axis=1)
    corner_source = jnp.stack(
        [portion[:, :, 0, -1], portion[:, :, 0, 0], portion[:, :, 3, -1], portion[:, :, 3, 0]],
        axis=2,
    )
    new_sides = jnp.einsum(
        "djn,fnjxc->fdjxc", side_choose, portion, preferred_element_type=jnp.float32
    )
    new_corners = jnp.einsum(
        "djn,fnjc->fdjc", corner_choose, corner_source, preferred_element_type=jnp.float32
    )
    return (new_sides.astype(jnp.bfloat16), new_corners.astype(jnp.bfloat16))


def empty_rims(frame_count, activation):
    tiles_dev, side_len, channels = (activation.shape[1], activation.shape[2], activation.shape[4])
    return (
        jnp.zeros((frame_count, tiles_dev, 4, side_len, channels), jnp.bfloat16),
        jnp.zeros((frame_count, tiles_dev, 4, channels), jnp.bfloat16),
    )


def assemble(longer, side_rims, corners):
    top_row = jnp.concatenate([corners[:, :, 0:1], side_rims[:, :, 0], corners[:, :, 1:2]], axis=2)
    bottom_row = jnp.concatenate(
        [corners[:, :, 2:3], side_rims[:, :, 3], corners[:, :, 3:4]], axis=2
    )
    middle = jnp.concatenate(
        [side_rims[:, :, 1][:, :, :, None], longer, side_rims[:, :, 2][:, :, :, None]], axis=3
    )
    return jnp.concatenate([top_row[:, :, None], middle, bottom_row[:, :, None]], axis=2)


def extend(activation, nearby):
    frames_dev = activation.shape[0]
    folder = partial(fold_edges, nearby=nearby)
    side_rims, corners = folder(
        empty_rims(frames_dev, activation),
        lax.all_gather(edge_pack(activation), "space", axis=1, tiled=True),
        jnp.int32(0),
    )
    prev_act, prev_sides, prev_corners = shifted(
        (activation[frames_dev - 2 :], side_rims[frames_dev - 2 :], corners[frames_dev - 2 :]),
        "tm",
        1,
    )
    longer = jnp.concatenate([prev_act, activation], axis=0)
    side_rims = jnp.concatenate([prev_sides, side_rims], axis=0)
    corners = jnp.concatenate([prev_corners, corners], axis=0)
    return assemble(longer, side_rims, corners)


def blank_tile(pieces, tile_valid):
    framed = pieces[0]
    return jnp.zeros(
        (framed.shape[0] - 2, framed.shape[1] - 2, framed.shape[2] - 2, framed.shape[3]),
        jnp.bfloat16,
    )


def home_tiles(inputs, home_valid, first_frame, worker):
    pieces = tuple((stacked[:, 0] for stacked in inputs))
    results = [lax.cond(home_valid[0] > first_frame, worker, blank_tile, pieces, home_valid[0])]
    return jnp.stack(results, axis=1)


def general_path(
    video_in,
    neighbours,
    valid_frames,
    norm1_gain,
    conv1_weight,
    conv1_bias,
    norm2_gain,
    conv2_weight,
    conv2_bias,
):
    frames_dev, tiles_dev, side_len, merged = video_in.shape
    channels = norm1_gain.shape[0]
    voxels = video_in.reshape(frames_dev, tiles_dev, side_len, side_len, channels)
    first_frame = lax.axis_index("tm") * frames_dev
    home_ids = lax.axis_index("space") * tiles_dev + jnp.arange(tiles_dev, dtype=jnp.int32)
    home_valid = jnp.take(valid_frames, home_ids)
    nearby = jnp.take(neighbours, home_ids, axis=0)
    frame_pos = first_frame + jnp.arange(frames_dev, dtype=jnp.int32)
    present = (frame_pos[:, None] < home_valid[None, :]).astype(jnp.bfloat16)
    masked = voxels * present[:, :, None, None, None]
    activation = norm_silu(masked.astype(jnp.float32), norm1_gain).astype(jnp.bfloat16)

    def frame_weights(tile_valid):
        return (frame_pos < tile_valid).astype(jnp.float32)[:, None, None, None]

    def first_worker(pieces, tile_valid):
        summed = conv_tile(pieces[0], conv1_weight)
        return norm_silu((summed + conv1_bias) * frame_weights(tile_valid), norm2_gain).astype(
            jnp.bfloat16
        )

    def second_worker(pieces, tile_valid):
        summed = conv_tile(pieces[0], conv2_weight)
        return (
            (summed + conv2_bias) * frame_weights(tile_valid) + pieces[1].astype(jnp.float32)
        ).astype(jnp.bfloat16)

    padded = extend(activation, nearby)
    hidden = home_tiles((padded,), home_valid, first_frame, first_worker)
    padded = extend(hidden, nearby)
    block_out = home_tiles((padded, masked), home_valid, first_frame, second_worker)
    return block_out.reshape(frames_dev, tiles_dev, side_len, side_len * channels)


LANE = 256


def silu(a):
    return a * (0.5 + 0.5 * jnp.tanh(0.5 * a))


def normed(v, gain):
    square = jnp.mean(v * v, axis=-1, keepdims=True)
    return silu(v * lax.rsqrt(square + epsilon) * gain)


def put(buf, x, f0, h):
    n, side, channels = h.shape
    row = lax.broadcasted_iota(jnp.int32, h.shape, 1)
    down = jnp.where(row == 0, 0.0, pltpu.roll(h, 1, 1))
    up = jnp.where(row == side - 1, 0.0, pltpu.roll(h, side - 1, 1))
    for q, t in enumerate((down, h, up)):
        buf[x, f0 : f0 + n, :, q * LANE : q * LANE + channels] = t.astype(jnp.bfloat16)


def zero_pads(buf, channels):
    columns, frames, side, _ = buf.shape
    zero = jnp.zeros((frames, side, LANE - channels), buf.dtype)

    def body(x, _):
        for q in range(3):
            buf[x, :, :, q * LANE + channels : (q + 1) * LANE] = zero
        return 0

    lax.fori_loop(0, columns, body, 0)


def spread_one(flat, weight, p, q):
    channels = weight.shape[2]
    zero = jnp.zeros((LANE - channels, channels), weight.dtype)
    turned = flat[3 * p + q].T
    for r in range(3):
        weight[p * 3 + r, q * LANE : q * LANE + channels] = turned[r * channels : (r + 1) * channels]
        weight[p * 3 + r, q * LANE + channels : (q + 1) * LANE] = zero


def spreads(flat, weight):
    return [partial(spread_one, flat, weight, p, q) for p in range(3) for q in range(3)]


def conv(buf, starts, width, f0, frames, weight, accs, beside=()):
    side, channels = buf.shape[2], weight.shape[2]
    totals = [None] * len(starts)
    done = 0
    for tap in range(9):
        p, r = divmod(tap, 3)
        for k, x0 in enumerate(starts):
            rows = buf[x0 + r : x0 + r + width, f0 + p : f0 + p + frames].reshape(-1, 3 * LANE)
            term = jnp.dot(rows, weight[tap], preferred_element_type=jnp.float32)
            totals[k] = term if totals[k] is None else totals[k] + term
        while done * 9 < len(beside) * (tap + 1):
            beside[done]()
            done += 1
    views = []
    for total, acc in zip(totals, accs):
        acc[0:width, 0:frames] = total.reshape(width, frames, side, channels)
        views += [acc.at[g, 0:frames] for g in range(width)]
    return views


def there(f0, frames, valid):
    frame = f0 + lax.broadcasted_iota(jnp.int32, (frames, 1, 1), 0)
    return ((frame >= 0) & (frame < valid)).astype(jnp.float32)


def act(buf, pair, f0, valid, x, at, gain):
    channels = gain.shape[1]
    values = pair.astype(jnp.float32) * there(f0, pair.shape[0], valid)
    for j in range(2):
        put(buf, x + j, at, normed(values[:, :, j * channels : (j + 1) * channels], gain))


def acts(buf, tile, f0, valid, at, gain):
    lanes = 2 * gain.shape[1]

    def one(k):
        act(buf, tile[:, :, k * lanes : (k + 1) * lanes], f0, valid, 2 + 2 * k, at, gain)

    return [partial(one, k) for k in range(tile.shape[2] // lanes)]


def row_of(ref):
    return ref[...].reshape(1, -1)


def hides(totals, buf, places, f0, at, bias, gain, valids):
    def one(g):
        total = totals[g][...]
        put(buf, places[g], at, normed((total + bias) * there(f0, total.shape[0], valids[g]), gain))

    return [partial(one, g) for g in range(len(places))]


def ended(totals, own, lanes, bias, f0, valid):
    parts = [total[...] + bias for total in totals]
    mask = there(f0, parts[0].shape[0], valid)
    both = jnp.concatenate([part * mask for part in parts], axis=-1)
    return (both + own[:, :, lanes].astype(jnp.float32) * mask).astype(jnp.bfloat16)


def finishes(totals, out, own, x0, bias, f0, valid):
    channels = bias.shape[1]

    def one(g):
        lanes = pl.ds((x0 + g) * channels, 2 * channels)
        out[:, :, lanes] = ended(totals[g : g + 2], own, lanes, bias, f0, valid)

    return [partial(one, g) for g in range(0, len(totals), 2)]


def run(works):
    for work in works:
        work()


def tile_kernel(nb, vf, own, gain1, buf1, buf2, flag):
    frames = own.shape[0]
    channels = gain1.shape[0]
    tiles = nb.shape[0]
    beyond = jnp.int32(0)
    for tile in range(tiles):
        for k in range(nb.shape[1]):
            if k not in (LEFT, RIGHT):
                beyond = jnp.maximum(beyond, tiles - nb[tile, k])
    flag[0] = beyond
    zero_pads(buf1, channels)
    zero_pads(buf2, channels)
    run(acts(buf1, own, lax.axis_index("tm") * frames, tracks(nb, vf)[0], frames, row_of(gain1)))


def late_kernel(nb, vf, buf1, flat1, flat2, bias1, gain2, _, weight1, weight2, buf2, acc):
    frames = buf1.shape[1] // 2
    inner = buf2.shape[0] - 4
    f0 = lax.axis_index("tm") * frames + 2
    valid = tracks(nb, vf)[0]
    run(spreads(flat1, weight1))
    totals = conv(buf1, (2,), inner, frames, frames - 2, weight1, (acc,), spreads(flat2, weight2))
    run(hides(totals, buf2, range(2, 2 + inner), f0, 4, row_of(bias1), row_of(gain2), [valid] * inner))


def main_kernel(nb, vf, own, prev, gain1, weight1, bias1, gain2, weight2, bias2, old1, old2, buf1, buf2, out, *accs):
    frames = prev.shape[0]
    columns = buf2.shape[0] - 2
    first = lax.axis_index("tm") * frames
    valid = tracks(nb, vf)[0]
    half = (columns - 4) // 2
    wide, rest = half + 2, columns - 4 - half
    before = acts(buf1, prev, first - frames, valid, 0, row_of(gain1))
    needed = (wide + 3) // 2
    norm = (first - 2, 0, row_of(bias1), row_of(gain2), [valid] * columns)
    run(before[:needed])
    totals = conv(buf1, (2,), wide, frames - 4, 4, weight1, accs[0:1], before[needed:])
    works = hides(totals, buf2, range(2, 2 + wide), *norm)
    totals = conv(buf1, (2 + wide,), rest, frames - 4, 4, weight1, accs[1:2], works)
    works = hides(totals, buf2, range(2 + wide, columns), *norm)
    totals = conv(buf2, (2,), half, 0, frames, weight2, accs[2:3], works)
    works = finishes(totals, out, own, 2, row_of(bias2), first, valid)
    totals = conv(buf2, (2 + half,), rest, 0, frames, weight2, accs[3:4], works)
    run(finishes(totals, out, own, 2 + half, row_of(bias2), first, valid))


def rim_kernel(nb, vf, own, rim, prev_rim, gain1, weight1, bias1, gain2, weight2, bias2, old1, old2, inner, buf1, buf2, out, *scratch):
    *accs, staged, sem = scratch
    frames, _, merged = own.shape
    columns = buf2.shape[0] - 2
    first = lax.axis_index("tm") * frames
    valid, left, right = tracks(nb, vf)
    for side, (x, v) in enumerate(((0, left), (columns + 2, right))):
        act(buf1, prev_rim[side], first - frames, v, x, 0, row_of(gain1))
        act(buf1, rim[side], first, v, x, frames, row_of(gain1))
    totals = conv(buf1, (0, columns), 2, frames - 4, frames + 2, weight1, accs[0:2])
    places = (0, 1, columns, columns + 1)
    run(hides(totals, buf2, places, first - 2, 0, row_of(bias1), row_of(gain2), (left, valid, valid, right)))
    totals = conv(buf2, (0, columns - 2), 2, 0, frames, weight2, accs[2:4])
    copies = []
    for side, lane in enumerate((0, merged - staged.shape[3])):
        lanes = pl.ds(lane, staged.shape[3])
        staged[side] = ended(totals[2 * side : 2 * side + 2], own, lanes, row_of(bias2), first, valid)
        copies.append(pltpu.make_async_copy(staged.at[side], out.at[:, :, lanes], sem.at[side]))
        copies[-1].start()
    for copy in copies:
        copy.wait()


LEFT, RIGHT = 3, 4


def tracks(nb, vf):
    me = lax.axis_index("space")
    tiles = nb.shape[0]

    def of(tile):
        return jnp.where(tile < tiles, vf[jnp.minimum(tile, tiles - 1)], 0)

    return vf[me], of(nb[me, LEFT]), of(nb[me, RIGHT])


def pick_kernel(nb, mine, pair, *outs):
    tiles = nb.shape[0]
    me = lax.axis_index("space")
    for step, out in enumerate(outs):
        there = lax.rem(me + 2 * (step + 1), tiles)
        for side, column in ((0, LEFT), (1, RIGHT)):
            source = nb[there, column]

            @pl.when(source == me)
            def _():
                out[side] = mine[1 - side]

            @pl.when(source != me)
            def _():
                out[side] = pair[1 - side]


def rims_kernel(nb, mine, pair, *rest):
    received, out = rest[:-1], rest[-1]
    tiles = nb.shape[0]
    half = tiles // 2
    me = lax.axis_index("space")
    for side, column in ((0, LEFT), (1, RIGHT)):
        source = nb[me, column]
        step = lax.rem(me // 2 - source // 2 + tiles, half)
        at_home = (step == 0) | (source >= tiles)

        @pl.when(at_home & (source == me ^ 1))
        def _():
            out[side] = pair[1 - side]

        @pl.when(at_home & (source != me ^ 1))
        def _():
            out[side] = mine[1 - side]

        for s, arrived in enumerate(received):

            @pl.when((step == s + 1) & (source < tiles))
            def _():
                out[side] = arrived[side]


def exchange(own, neighbours, channels):
    count = lax.axis_size("space")
    vmem = pl.BlockSpec(memory_space=pltpu.VMEM)
    smem = pl.BlockSpec(memory_space=pltpu.SMEM)
    mine = jnp.stack([own[:, :, : 2 * channels], own[:, :, -2 * channels :]])
    pair = lax.ppermute(mine, "space", [(i, i ^ 1) for i in range(count)])
    piece = jax.ShapeDtypeStruct(mine.shape, mine.dtype)
    steps = count // 2 - 1
    sent = pl.pallas_call(
        pick_kernel,
        out_shape=[piece] * steps,
        in_specs=[smem, vmem, vmem],
        out_specs=[vmem] * steps,
        compiler_params=pltpu.CompilerParams(vmem_limit_bytes=8 * 2**20),
    )(neighbours, mine, pair)
    received = [
        lax.ppermute(value, "space", [(i, (i + 2 * (s + 1)) % count) for i in range(count)])
        for s, value in enumerate(sent)
    ]
    return pl.pallas_call(
        rims_kernel,
        out_shape=piece,
        in_specs=[smem] + [vmem] * (2 + steps),
        out_specs=vmem,
        compiler_params=pltpu.CompilerParams(vmem_limit_bytes=8 * 2**20),
    )(neighbours, mine, pair, *received)


def call(kernel, cost, outs, ins, args, places=None, **more):
    flops, moved = cost
    return pl.pallas_call(
        kernel,
        out_shape=outs,
        in_specs=ins,
        out_specs=[VM] * len(outs) if places is None else places,
        cost_estimate=pl.CostEstimate(flops=flops, bytes_accessed=moved, transcendentals=0),
        compiler_params=pltpu.CompilerParams(vmem_limit_bytes=24 * 2**20),
        **more,
    )(*args)


VM = pl.BlockSpec(memory_space=pltpu.VMEM)
SM = pl.BlockSpec(memory_space=pltpu.SMEM)
HB = pl.BlockSpec(memory_space=pl.ANY)


def rooms(side, channels):
    def room(width, frames):
        return pltpu.VMEM((width, frames, side, channels), jnp.float32)

    return room


def row_path(video_in, neighbours, valid_frames, gain1, weight1, bias1, gain2, weight2, bias2):
    own = video_in[:, 0]
    frames, side, merged = own.shape
    channels = gain1.shape[0]
    columns = merged // channels
    tables = (neighbours, valid_frames)
    prev = shifted(own, "tm", 1)
    rim = exchange(own, neighbours, channels)
    prev_rim = shifted(rim, "tm", 1)
    room = rooms(side, channels)
    one = 2 * 27 * channels * channels * side
    space1 = pltpu.VMEM((columns + 4, 2 * frames, side, 3 * LANE), jnp.bfloat16)
    space2 = pltpu.VMEM((columns + 2, frames + 2, side, 3 * LANE), jnp.bfloat16)
    spaced = pltpu.VMEM((9, 3 * LANE, channels), jnp.bfloat16)
    buf1, buf2, flag = call(
        tile_kernel,
        (one * 2 * columns, own.size),
        [space1, space2, jax.ShapeDtypeStruct((1,), jnp.int32)],
        [SM, SM, VM, VM],
        (*tables, own, gain1),
        places=[VM, VM, SM],
    )
    wide1, wide2, buf2 = call(
        late_kernel,
        (one * 4 * columns, own.size),
        [spaced, spaced, space2],
        [SM, SM] + [VM] * 6,
        (*tables, buf1, jnp.swapaxes(weight1, 1, 2), jnp.swapaxes(weight2, 1, 2), bias1, gain2, buf2),
        input_output_aliases={7: 2},
        scratch_shapes=[room(columns - 2, frames - 2)],
    )
    buf1, buf2, inner = call(
        main_kernel,
        (one * 8 * columns, own.size),
        [space1, space2, jax.ShapeDtypeStruct(own.shape, own.dtype)],
        [SM, SM] + [VM] * 10,
        (*tables, own, prev, gain1, wide1, bias1, gain2, wide2, bias2, buf1, buf2),
        input_output_aliases={10: 0, 11: 1},
        scratch_shapes=[room(columns // 2, 4)] * 2 + [room(columns // 2, frames)] * 2,
    )
    return flag, (own, rim, prev_rim, wide1, wide2, buf1, buf2, inner)


def row_end(state, tables, gain1, bias1, gain2, bias2):
    own, rim, prev_rim, wide1, wide2, buf1, buf2, inner = state
    space1, space2 = pltpu.VMEM(buf1.shape, buf1.dtype), pltpu.VMEM(buf2.shape, buf2.dtype)
    room = rooms(own.shape[1], gain1.shape[0])
    _, _, out = call(
        rim_kernel,
        (own.size * 1000, own.size),
        [space1, space2, jax.ShapeDtypeStruct(own.shape, own.dtype)],
        [SM, SM] + [VM] * 11 + [HB],
        (*tables, own, rim, prev_rim, gain1, wide1, bias1, gain2, wide2, bias2, buf1, buf2, inner),
        places=[VM, VM, HB],
        input_output_aliases={11: 0, 12: 1, 13: 2},
        scratch_shapes=[room(2, own.shape[0] + 2)] * 4 + [pltpu.VMEM(rim.shape, rim.dtype), pltpu.SemaphoreType.DMA((2,))],
    )
    return out[:, None]


def on_device(*args):
    video_in, neighbours, valid_frames, gain1, weight1, bias1, gain2, weight2, bias2 = args
    frames_dev, tiles_dev = video_in.shape[:2]
    tiles = neighbours.shape[0]
    if tiles_dev != 1 or tiles % 2 or frames_dev != 4:
        return general_path(*args)
    flag, state = row_path(*args)
    return lax.cond(
        flag[0] > 0,
        lambda state, args: general_path(*args),
        lambda state, args: row_end(state, args[1:3], gain1, bias1, gain2, bias2),
        state,
        args,
    )


def solution(mesh):
    in_specs = (P("tm", "space", None, None), P(), P(), P(), P(), P(), P(), P(), P())
    out_specs = P("tm", "space", None, None)
    return jax.shard_map(
        on_device, mesh=mesh, in_specs=in_specs, out_specs=out_specs, check_vma=False
    )
```

```python
from functools import partial

import jax
import jax.numpy as jnp
from jax import lax
from jax.experimental import pallas as pl
from jax.experimental.pallas import tpu as pltpu
from jax.sharding import PartitionSpec as P

epsilon = 1e-06


def shifted(value, axis, steps):
    count = lax.axis_size(axis)
    first, last = (max(0, -steps), min(count, count - steps))
    return lax.ppermute(value, axis, [(source, source + steps) for source in range(first, last)])


def norm_silu(values, scale_gain):
    square = jnp.mean(values * values, axis=-1, keepdims=True)
    return jax.nn.silu(values * lax.rsqrt(square + epsilon) * scale_gain)


def conv_tile(framed, weight):
    frames_out = framed.shape[0] - 2
    side_len = framed.shape[1] - 2
    channels = framed.shape[-1]
    widened = jnp.concatenate(
        [framed[:, :, col_off : col_off + side_len] for col_off in range(3)], axis=-1
    )

    def tap(index, summed):
        start = (index // 3, index % 3, 0, 0)
        window = lax.dynamic_slice(widened, start, (frames_out, side_len, side_len, 3 * channels))
        taps = lax.dynamic_index_in_dim(weight, index, 0, keepdims=False)
        return summed + jnp.dot(window.reshape(-1, 3 * channels), taps, preferred_element_type=jnp.float32)

    summed = lax.fori_loop(0, 9, tap, jnp.zeros((frames_out * side_len * side_len, channels), jnp.float32))
    return summed.reshape(frames_out, side_len, side_len, channels)


def edge_pack(activation):
    return jnp.stack(
        [
            activation[:, :, -1],
            activation[:, :, :, -1],
            activation[:, :, :, 0],
            activation[:, :, 0],
        ],
        axis=2,
    )


def fold_edges(totals, portion, offset, nearby):
    amount = portion.shape[1]
    tile_ids = jnp.arange(amount, dtype=jnp.int32)
    choose = (nearby[:, :, None] == tile_ids[None, None, :]).astype(jnp.bfloat16)
    side_choose = jnp.stack([choose[:, 1], choose[:, 3], choose[:, 4], choose[:, 6]], axis=1)
    corner_choose = jnp.stack([choose[:, 0], choose[:, 2], choose[:, 5], choose[:, 7]], axis=1)
    corner_source = jnp.stack(
        [portion[:, :, 0, -1], portion[:, :, 0, 0], portion[:, :, 3, -1], portion[:, :, 3, 0]],
        axis=2,
    )
    new_sides = jnp.einsum(
        "djn,fnjxc->fdjxc", side_choose, portion, preferred_element_type=jnp.float32
    )
    new_corners = jnp.einsum(
        "djn,fnjc->fdjc", corner_choose, corner_source, preferred_element_type=jnp.float32
    )
    return (new_sides.astype(jnp.bfloat16), new_corners.astype(jnp.bfloat16))


def empty_rims(frame_count, activation):
    tiles_dev, side_len, channels = (activation.shape[1], activation.shape[2], activation.shape[4])
    return (
        jnp.zeros((frame_count, tiles_dev, 4, side_len, channels), jnp.bfloat16),
        jnp.zeros((frame_count, tiles_dev, 4, channels), jnp.bfloat16),
    )


def assemble(longer, side_rims, corners):
    top_row = jnp.concatenate([corners[:, :, 0:1], side_rims[:, :, 0], corners[:, :, 1:2]], axis=2)
    bottom_row = jnp.concatenate(
        [corners[:, :, 2:3], side_rims[:, :, 3], corners[:, :, 3:4]], axis=2
    )
    middle = jnp.concatenate(
        [side_rims[:, :, 1][:, :, :, None], longer, side_rims[:, :, 2][:, :, :, None]], axis=3
    )
    return jnp.concatenate([top_row[:, :, None], middle, bottom_row[:, :, None]], axis=2)


def extend(activation, nearby):
    frames_dev = activation.shape[0]
    folder = partial(fold_edges, nearby=nearby)
    side_rims, corners = folder(
        empty_rims(frames_dev, activation),
        lax.all_gather(edge_pack(activation), "space", axis=1, tiled=True),
        jnp.int32(0),
    )
    prev_act, prev_sides, prev_corners = shifted(
        (activation[frames_dev - 2 :], side_rims[frames_dev - 2 :], corners[frames_dev - 2 :]),
        "tm",
        1,
    )
    longer = jnp.concatenate([prev_act, activation], axis=0)
    side_rims = jnp.concatenate([prev_sides, side_rims], axis=0)
    corners = jnp.concatenate([prev_corners, corners], axis=0)
    return assemble(longer, side_rims, corners)


def blank_tile(pieces, tile_valid):
    framed = pieces[0]
    return jnp.zeros(
        (framed.shape[0] - 2, framed.shape[1] - 2, framed.shape[2] - 2, framed.shape[3]),
        jnp.bfloat16,
    )


def home_tiles(inputs, home_valid, first_frame, worker):
    pieces = tuple((stacked[:, 0] for stacked in inputs))
    results = [lax.cond(home_valid[0] > first_frame, worker, blank_tile, pieces, home_valid[0])]
    return jnp.stack(results, axis=1)


def general_path(
    video_in,
    neighbours,
    valid_frames,
    norm1_gain,
    conv1_weight,
    conv1_bias,
    norm2_gain,
    conv2_weight,
    conv2_bias,
):
    frames_dev, tiles_dev, side_len, _ = video_in.shape
    channels = norm1_gain.shape[0]
    voxels = video_in.reshape(frames_dev, tiles_dev, side_len, side_len, channels)
    first_frame = lax.axis_index("tm") * frames_dev
    home_ids = lax.axis_index("space") * tiles_dev + jnp.arange(tiles_dev, dtype=jnp.int32)
    home_valid = jnp.take(valid_frames, home_ids)
    nearby = jnp.take(neighbours, home_ids, axis=0)
    frame_pos = first_frame + jnp.arange(frames_dev, dtype=jnp.int32)
    present = (frame_pos[:, None] < home_valid[None, :]).astype(jnp.bfloat16)
    masked = voxels * present[:, :, None, None, None]
    activation = norm_silu(masked.astype(jnp.float32), norm1_gain).astype(jnp.bfloat16)

    def frame_weights(tile_valid):
        return (frame_pos < tile_valid).astype(jnp.float32)[:, None, None, None]

    def first_worker(pieces, tile_valid):
        summed = conv_tile(pieces[0], conv1_weight)
        return norm_silu((summed + conv1_bias) * frame_weights(tile_valid), norm2_gain).astype(
            jnp.bfloat16
        )

    def second_worker(pieces, tile_valid):
        summed = conv_tile(pieces[0], conv2_weight)
        return (
            (summed + conv2_bias) * frame_weights(tile_valid) + pieces[1].astype(jnp.float32)
        ).astype(jnp.bfloat16)

    padded = extend(activation, nearby)
    hidden = home_tiles((padded,), home_valid, first_frame, first_worker)
    padded = extend(hidden, nearby)
    block_out = home_tiles((padded, masked), home_valid, first_frame, second_worker)
    return block_out.reshape(frames_dev, tiles_dev, side_len, side_len * channels)


LANE = 256


def normed(v, half_gain, mask):
    square = jnp.mean(v * v, axis=-1, keepdims=True)
    u = v * (lax.rsqrt(square + epsilon) * mask) * half_gain
    return u + u * jnp.tanh(u)


def put(buf, x, f0, h):
    n, side, channels = h.shape
    row = lax.broadcasted_iota(jnp.int32, h.shape, 1)
    down = jnp.where(row == 0, 0.0, pltpu.roll(h, 1, 1))
    up = jnp.where(row == side - 1, 0.0, pltpu.roll(h, side - 1, 1))
    zero = jnp.zeros((n, side, LANE - channels), jnp.bfloat16)
    for q, t in enumerate((down, h, up)):
        buf[x, f0 : f0 + n, :, q * LANE : q * LANE + channels] = t.astype(jnp.bfloat16)
        buf[x, f0 : f0 + n, :, q * LANE + channels : (q + 1) * LANE] = zero


def spread_one(flat, weight, p, q):
    channels = weight.shape[2]
    zero = jnp.zeros((LANE - channels, channels), weight.dtype)
    turned = flat[3 * p + q].T
    for r in range(3):
        weight[p * 3 + r, q * LANE : q * LANE + channels] = turned[r * channels : (r + 1) * channels]
        weight[p * 3 + r, q * LANE + channels : (q + 1) * LANE] = zero


def spreads(flat, weight):
    return [partial(spread_one, flat, weight, p, q) for p in range(3) for q in range(3)]


def conv(buf, starts, width, f0, frames, weight, accs, beside=()):
    side, channels = buf.shape[2], weight.shape[2]
    totals = [None] * len(starts)
    done = 0
    for tap in range(9):
        p, r = divmod(tap, 3)
        for k, x0 in enumerate(starts):
            rows = buf[x0 + r : x0 + r + width, f0 + p : f0 + p + frames].reshape(-1, 3 * LANE)
            term = jnp.dot(rows, weight[tap], preferred_element_type=jnp.float32)
            totals[k] = term if totals[k] is None else totals[k] + term
        while done * 9 < len(beside) * (tap + 1):
            beside[done]()
            done += 1
    views = []
    for total, acc in zip(totals, accs):
        acc[0:width, 0:frames] = total.reshape(width, frames, side, channels)
        views += [acc.at[g, 0:frames] for g in range(width)]
    return views


def there(f0, frames, valid):
    frame = f0 + lax.broadcasted_iota(jnp.int32, (frames, 1, 1), 0)
    return ((frame >= 0) & (frame < valid)).astype(jnp.float32)


def act(buf, pair, mask, x, at, gain):
    channels = gain.shape[1]
    values = pair.astype(jnp.float32)
    for j in range(2):
        put(buf, x + j, at, normed(values[:, :, j * channels : (j + 1) * channels], gain, mask))


def acts(buf, tile, mask, at, gain):
    lanes = 2 * gain.shape[1]

    def one(k):
        act(buf, tile[:, :, k * lanes : (k + 1) * lanes], mask, 2 + 2 * k, at, gain)

    return [partial(one, k) for k in range(tile.shape[2] // lanes)]


def row_of(ref):
    return ref[...].reshape(1, -1)


def hides(totals, buf, places, at, bias, gain, masks):
    def one(g):
        total = totals[g][...]
        put(buf, places[g], at, normed(total + bias, gain, masks[g]))

    return [partial(one, g) for g in range(len(places))]


def ended(totals, own, lanes, bias, mask):
    parts = [total[...] + bias for total in totals]
    both = jnp.concatenate([part * mask for part in parts], axis=-1)
    return (both + own[:, :, lanes].astype(jnp.float32) * mask).astype(jnp.bfloat16)


def finishes(totals, out, own, x0, at, bias, mask):
    channels = bias.shape[1]

    def one(g):
        lanes = pl.ds((x0 + g) * channels, 2 * channels)
        out[:, :, pl.ds((at + g) * channels, 2 * channels)] = ended(totals[g : g + 2], own, lanes, bias, mask)

    return [partial(one, g) for g in range(0, len(totals), 2)]


def run(works):
    for work in works:
        work()


def load_kernel(far, own, mine, sem):
    lanes = mine.shape[3]
    copies = [
        pltpu.make_async_copy(far.at[:, :, pl.ds(0, lanes)], mine.at[0], sem.at[0]),
        pltpu.make_async_copy(far.at[:, :, pl.ds(far.shape[2] - lanes, lanes)], mine.at[1], sem.at[1]),
        pltpu.make_async_copy(far, own, sem.at[2]),
    ]
    for copy in copies:
        copy.start()
    for copy in copies:
        copy.wait()


def tile_kernel(nb, vf, own, gain1, far1, far2, buf1, mask, flat1, flat2, sem):
    frames = own.shape[0]
    copies = [pltpu.make_async_copy(far1, flat1, sem.at[0]), pltpu.make_async_copy(far2, flat2, sem.at[1])]
    for copy in copies:
        copy.start()
    first, valid = lax.axis_index("tm") * frames, tracks(nb, vf)[0]
    frame = first - frames + lax.broadcasted_iota(jnp.int32, mask.shape, 0)
    mask[...] = ((frame >= 0) & (frame < valid)).astype(jnp.float32)
    run(acts(buf1, own, there(first, frames, valid), frames, 0.5 * row_of(gain1)))
    for copy in copies:
        copy.wait()


def late_kernel(mask, buf1, flat1, flat2, bias1, gain2, nb, weight1, weight2, buf2, flag, acc):
    k = lax.broadcasted_iota(jnp.int32, nb.shape, 1)
    beyond = jnp.where((k < LEFT) | (k > RIGHT), nb.shape[0] - nb[...], 0)
    flag[0] = jnp.max(beyond)
    frames = buf1.shape[1] // 2
    inner = buf2.shape[0] - 4
    run(spreads(flat1, weight1))
    works = spreads(flat2, weight2)
    totals = conv(buf1, (2,), inner, frames, frames - 2, weight1, (acc,), works)
    masks = [mask[frames + 2 :, :, :1]] * inner
    run(hides(totals, buf2, range(2, 2 + inner), 4, row_of(bias1), 0.5 * row_of(gain2), masks))


def split_of(columns):
    half = (columns - 4) // 2
    return half, half + 2, columns - 4 - half


def early_kernel(mask, prev, gain1, weight1, old1, buf1, acc):
    frames = prev.shape[0]
    _, wide, _ = split_of(prev.shape[2] // gain1.shape[0])
    before = acts(buf1, prev, mask[:frames, :, :1], 0, 0.5 * row_of(gain1))
    needed = (wide + 3) // 2
    run(before[:needed])
    conv(buf1, (2,), wide, frames - 4, 4, weight1, (acc,), before[needed:])


def main_kernel(mask, own, buf1, acc, weight1, bias1, gain2, weight2, bias2, old2, buf2, out, *accs):
    frames = own.shape[0]
    columns = buf2.shape[0] - 2
    half, wide, rest = split_of(columns)
    norm = (0, row_of(bias1), 0.5 * row_of(gain2), [mask[frames - 2 : frames + 2, :, :1]] * columns)
    present = mask[frames:, :, :1]
    works = hides([acc.at[g] for g in range(wide)], buf2, range(2, 2 + wide), *norm)
    totals = conv(buf1, (2 + wide,), rest, frames - 4, 4, weight1, accs[0:1], works)
    works = hides(totals, buf2, range(2 + wide, columns), *norm)
    totals = conv(buf2, (2,), half, 0, frames, weight2, accs[1:2], works)
    works = finishes(totals, out, own, 2, 0, row_of(bias2), present)
    totals = conv(buf2, (2 + half,), rest, 0, frames, weight2, accs[2:3], works)
    run(finishes(totals, out, own, 2 + half, half, row_of(bias2), present))


def rim_kernel(nb, vf, own, rim, prev_rim, gain1, weight1, bias1, gain2, weight2, bias2, old1, old2, inner, buf1, buf2, out, *scratch):
    *accs, staged, sem = scratch
    frames, _, merged = own.shape
    columns = buf2.shape[0] - 2
    first = lax.axis_index("tm") * frames
    valid, left, right = tracks(nb, vf)
    ends = staged.shape[3]
    copies = [pltpu.make_async_copy(inner, out.at[:, :, pl.ds(ends, merged - 2 * ends)], sem.at[2])]
    copies[0].start()
    for side, (x, v) in enumerate(((0, left), (columns + 2, right))):
        act(buf1, prev_rim[side], there(first - frames, frames, v), x, 0, 0.5 * row_of(gain1))
        act(buf1, rim[side], there(first, frames, v), x, frames, 0.5 * row_of(gain1))
    totals = conv(buf1, (0, columns), 2, frames - 4, frames + 2, weight1, accs[0:2])
    places = (0, 1, columns, columns + 1)
    masks = [there(first - 2, frames + 2, v) for v in (left, valid, valid, right)]
    run(hides(totals, buf2, places, 0, row_of(bias1), 0.5 * row_of(gain2), masks))
    totals = conv(buf2, (0, columns - 2), 2, 0, frames, weight2, accs[2:4])
    for side, lane in enumerate((0, merged - ends)):
        lanes = pl.ds(lane, ends)
        staged[side] = ended(totals[2 * side : 2 * side + 2], own, lanes, row_of(bias2), there(first, frames, valid))
        copies.append(pltpu.make_async_copy(staged.at[side], out.at[:, :, lanes], sem.at[side]))
        copies[-1].start()
    for copy in copies:
        copy.wait()


LEFT, RIGHT = 3, 4


def tracks(nb, vf):
    me = lax.axis_index("space")
    tiles = nb.shape[0]

    def of(tile):
        return jnp.where(tile < tiles, vf[jnp.minimum(tile, tiles - 1)], 0)

    return vf[me], of(nb[me, LEFT]), of(nb[me, RIGHT])


def pick_kernel(nb, mine, pair, *outs):
    tiles = nb.shape[0]
    me = lax.axis_index("space")
    for step, out in enumerate(outs):
        there = lax.rem(me + 2 * (step + 1), tiles)
        for side, column in ((0, LEFT), (1, RIGHT)):
            source = nb[there, column]

            @pl.when(source == me)
            def _():
                out[side] = mine[1 - side]

            @pl.when(source != me)
            def _():
                out[side] = pair[1 - side]


def rims_kernel(nb, mine, pair, *rest):
    received, out = rest[:-1], rest[-1]
    tiles = nb.shape[0]
    half = tiles // 2
    me = lax.axis_index("space")
    for side, column in ((0, LEFT), (1, RIGHT)):
        source = nb[me, column]
        step = lax.rem(me // 2 - source // 2 + tiles, half)
        at_home = (step == 0) | (source >= tiles)

        @pl.when(at_home & (source == me ^ 1))
        def _():
            out[side] = pair[1 - side]

        @pl.when(at_home & (source != me ^ 1))
        def _():
            out[side] = mine[1 - side]

        for s, arrived in enumerate(received):

            @pl.when((step == s + 1) & (source < tiles))
            def _():
                out[side] = arrived[side]


def exchange(own, mine, neighbours):
    count = lax.axis_size("space")
    vmem = pl.BlockSpec(memory_space=pltpu.VMEM)
    smem = pl.BlockSpec(memory_space=pltpu.SMEM)
    pair = lax.ppermute(mine, "space", [(i, i ^ 1) for i in range(count)])
    piece = jax.ShapeDtypeStruct(mine.shape, mine.dtype)
    steps = count // 2 - 1
    sent = pl.pallas_call(
        pick_kernel,
        out_shape=[piece] * steps,
        in_specs=[smem, vmem, vmem],
        out_specs=[vmem] * steps,
        compiler_params=pltpu.CompilerParams(vmem_limit_bytes=8 * 2**20),
    )(neighbours, mine, pair)
    received = []
    for s, value in enumerate(sent):
        received.append(lax.ppermute(value, "space", [(i, (i + 2 * (s + 1)) % count) for i in range(count)]))
    prev = shifted(own, "tm", 1)
    rim = pl.pallas_call(
        rims_kernel,
        out_shape=piece,
        in_specs=[smem] + [vmem] * (2 + steps),
        out_specs=vmem,
        compiler_params=pltpu.CompilerParams(vmem_limit_bytes=8 * 2**20),
    )(neighbours, mine, pair, *received)
    return prev, rim


def call(kernel, cost, outs, ins, args, places=None, **more):
    flops, moved = cost
    return pl.pallas_call(
        kernel,
        out_shape=outs,
        in_specs=ins,
        out_specs=[VM] * len(outs) if places is None else places,
        cost_estimate=pl.CostEstimate(flops=flops, bytes_accessed=moved, transcendentals=0),
        compiler_params=pltpu.CompilerParams(vmem_limit_bytes=24 * 2**20),
        **more,
    )(*args)


VM = pl.BlockSpec(memory_space=pltpu.VMEM)
SM = pl.BlockSpec(memory_space=pltpu.SMEM)
HB = pl.BlockSpec(memory_space=pl.ANY)


def rooms(side, channels):
    def room(width, frames):
        return pltpu.VMEM((width, frames, side, channels), jnp.float32)

    return room


def row_path(video_in, neighbours, valid_frames, gain1, weight1, bias1, gain2, weight2, bias2):
    far = video_in[:, 0]
    frames, side, merged = far.shape
    channels = gain1.shape[0]
    columns = merged // channels
    tables = (neighbours, valid_frames)
    room = rooms(side, channels)
    one = 2 * 27 * channels * channels * side
    flat = pltpu.VMEM((9, channels, 3 * channels), jnp.bfloat16)
    own, mine = call(
        load_kernel,
        (one, far.size),
        [pltpu.VMEM(far.shape, far.dtype), pltpu.VMEM((2, frames, side, 2 * channels), far.dtype)],
        [HB],
        (far,),
        scratch_shapes=[pltpu.SemaphoreType.DMA((3,))],
    )
    prev, rim = exchange(far, mine, neighbours)
    prev_rim = shifted(rim, "tm", 1)
    space1 = pltpu.VMEM((columns + 4, 2 * frames, side, 3 * LANE), jnp.bfloat16)
    space2 = pltpu.VMEM((columns + 2, frames + 2, side, 3 * LANE), jnp.bfloat16)
    spaced = pltpu.VMEM((9, 3 * LANE, channels), jnp.bfloat16)
    buf1, mask, flat1, flat2 = call(
        tile_kernel,
        (one * 2 * columns, own.size),
        [space1, pltpu.VMEM((2 * frames, side, 128), jnp.float32), flat, flat],
        [SM, SM, VM, VM, HB, HB],
        (*tables, own, gain1, jnp.swapaxes(weight1, 1, 2), jnp.swapaxes(weight2, 1, 2)),
        scratch_shapes=[pltpu.SemaphoreType.DMA((2,))],
    )
    wide1, wide2, buf2, flag = call(
        late_kernel,
        (one * 4 * columns, own.size),
        [spaced, spaced, space2, jax.ShapeDtypeStruct((1,), jnp.int32)],
        [VM] * 7,
        (mask, buf1, flat1, flat2, bias1, gain2, neighbours),
        places=[VM] * 3 + [SM],
        scratch_shapes=[room(columns - 2, frames - 2)],
    )
    buf1, acc = call(
        early_kernel,
        (one * 3 * columns, own.size),
        [space1, room(split_of(columns)[1], 4)],
        [VM] * 5,
        (mask, prev, gain1, wide1, buf1),
        input_output_aliases={4: 0},
    )
    buf2, inner = call(
        main_kernel,
        (one * 8 * columns, own.size),
        [space2, pltpu.VMEM((frames, side, (columns - 4) * channels), own.dtype)],
        [VM] * 10,
        (mask, own, buf1, acc, wide1, bias1, gain2, wide2, bias2, buf2),
        input_output_aliases={9: 0},
        scratch_shapes=[room(columns // 2, 4)] + [room(columns // 2, frames)] * 2,
    )
    return flag, (own, rim, prev_rim, wide1, wide2, buf1, buf2, inner)


def row_end(state, tables, gain1, bias1, gain2, bias2):
    own, rim, prev_rim, wide1, wide2, buf1, buf2, inner = state
    space1, space2 = pltpu.VMEM(buf1.shape, buf1.dtype), pltpu.VMEM(buf2.shape, buf2.dtype)
    room = rooms(own.shape[1], gain1.shape[0])
    _, _, out = call(
        rim_kernel,
        (own.size * 1000, own.size),
        [space1, space2, jax.ShapeDtypeStruct(own.shape, own.dtype)],
        [SM, SM] + [VM] * 12,
        (*tables, own, rim, prev_rim, gain1, wide1, bias1, gain2, wide2, bias2, buf1, buf2, inner),
        places=[VM, VM, HB],
        input_output_aliases={11: 0, 12: 1},
        scratch_shapes=[room(2, own.shape[0] + 2)] * 4 + [pltpu.VMEM(rim.shape, rim.dtype), pltpu.SemaphoreType.DMA((3,))],
    )
    return out[:, None]


def on_device(*args):
    video_in, neighbours, _, gain1, _, bias1, gain2, _, bias2 = args
    frames_dev, tiles_dev = video_in.shape[:2]
    tiles = neighbours.shape[0]
    if tiles_dev != 1 or tiles % 2 or frames_dev != 4:
        return general_path(*args)
    flag, state = row_path(*args)
    return lax.cond(
        flag[0] > 0,
        lambda state, args: general_path(*args),
        lambda state, args: row_end(state, args[1:3], gain1, bias1, gain2, bias2),
        state,
        args,
    )


def solution(mesh):
    in_specs = (P("tm", "space", None, None), P(), P(), P(), P(), P(), P(), P(), P())
    out_specs = P("tm", "space", None, None)
    return jax.shard_map(
        on_device, mesh=mesh, in_specs=in_specs, out_specs=out_specs, check_vma=False
    )
```

```python
from functools import partial

import jax
import jax.numpy as jnp
from jax import lax
from jax.experimental import pallas as pl
from jax.experimental.pallas import tpu as pltpu
from jax.sharding import PartitionSpec as P

epsilon = 1e-06


def shifted(value, axis, steps):
    count = lax.axis_size(axis)
    first, last = (max(0, -steps), min(count, count - steps))
    return lax.ppermute(value, axis, [(source, source + steps) for source in range(first, last)])


def norm_silu(values, scale_gain):
    square = jnp.mean(values * values, axis=-1, keepdims=True)
    return jax.nn.silu(values * lax.rsqrt(square + epsilon) * scale_gain)


def conv_tile(framed, weight):
    frames_out = framed.shape[0] - 2
    side_len = framed.shape[1] - 2
    channels = framed.shape[-1]
    widened = jnp.concatenate(
        [framed[:, :, col_off : col_off + side_len] for col_off in range(3)], axis=-1
    )

    def tap(index, summed):
        start = (index // 3, index % 3, 0, 0)
        window = lax.dynamic_slice(widened, start, (frames_out, side_len, side_len, 3 * channels))
        taps = lax.dynamic_index_in_dim(weight, index, 0, keepdims=False)
        return summed + jnp.dot(window.reshape(-1, 3 * channels), taps, preferred_element_type=jnp.float32)

    summed = lax.fori_loop(0, 9, tap, jnp.zeros((frames_out * side_len * side_len, channels), jnp.float32))
    return summed.reshape(frames_out, side_len, side_len, channels)


def edge_pack(activation):
    return jnp.stack(
        [
            activation[:, :, -1],
            activation[:, :, :, -1],
            activation[:, :, :, 0],
            activation[:, :, 0],
        ],
        axis=2,
    )


def fold_edges(totals, portion, offset, nearby):
    amount = portion.shape[1]
    tile_ids = jnp.arange(amount, dtype=jnp.int32)
    choose = (nearby[:, :, None] == tile_ids[None, None, :]).astype(jnp.bfloat16)
    side_choose = jnp.stack([choose[:, 1], choose[:, 3], choose[:, 4], choose[:, 6]], axis=1)
    corner_choose = jnp.stack([choose[:, 0], choose[:, 2], choose[:, 5], choose[:, 7]], axis=1)
    corner_source = jnp.stack(
        [portion[:, :, 0, -1], portion[:, :, 0, 0], portion[:, :, 3, -1], portion[:, :, 3, 0]],
        axis=2,
    )
    new_sides = jnp.einsum(
        "djn,fnjxc->fdjxc", side_choose, portion, preferred_element_type=jnp.float32
    )
    new_corners = jnp.einsum(
        "djn,fnjc->fdjc", corner_choose, corner_source, preferred_element_type=jnp.float32
    )
    return (new_sides.astype(jnp.bfloat16), new_corners.astype(jnp.bfloat16))


def empty_rims(frame_count, activation):
    tiles_dev, side_len, channels = (activation.shape[1], activation.shape[2], activation.shape[4])
    return (
        jnp.zeros((frame_count, tiles_dev, 4, side_len, channels), jnp.bfloat16),
        jnp.zeros((frame_count, tiles_dev, 4, channels), jnp.bfloat16),
    )


def assemble(longer, side_rims, corners):
    top_row = jnp.concatenate([corners[:, :, 0:1], side_rims[:, :, 0], corners[:, :, 1:2]], axis=2)
    bottom_row = jnp.concatenate(
        [corners[:, :, 2:3], side_rims[:, :, 3], corners[:, :, 3:4]], axis=2
    )
    middle = jnp.concatenate(
        [side_rims[:, :, 1][:, :, :, None], longer, side_rims[:, :, 2][:, :, :, None]], axis=3
    )
    return jnp.concatenate([top_row[:, :, None], middle, bottom_row[:, :, None]], axis=2)


def extend(activation, nearby):
    frames_dev = activation.shape[0]
    folder = partial(fold_edges, nearby=nearby)
    side_rims, corners = folder(
        empty_rims(frames_dev, activation),
        lax.all_gather(edge_pack(activation), "space", axis=1, tiled=True),
        jnp.int32(0),
    )
    prev_act, prev_sides, prev_corners = shifted(
        (activation[frames_dev - 2 :], side_rims[frames_dev - 2 :], corners[frames_dev - 2 :]),
        "tm",
        1,
    )
    longer = jnp.concatenate([prev_act, activation], axis=0)
    side_rims = jnp.concatenate([prev_sides, side_rims], axis=0)
    corners = jnp.concatenate([prev_corners, corners], axis=0)
    return assemble(longer, side_rims, corners)


def blank_tile(pieces, tile_valid):
    framed = pieces[0]
    return jnp.zeros(
        (framed.shape[0] - 2, framed.shape[1] - 2, framed.shape[2] - 2, framed.shape[3]),
        jnp.bfloat16,
    )


def home_tiles(inputs, home_valid, first_frame, worker):
    pieces = tuple((stacked[:, 0] for stacked in inputs))
    results = [lax.cond(home_valid[0] > first_frame, worker, blank_tile, pieces, home_valid[0])]
    return jnp.stack(results, axis=1)


def general_path(
    video_in,
    neighbours,
    valid_frames,
    norm1_gain,
    conv1_weight,
    conv1_bias,
    norm2_gain,
    conv2_weight,
    conv2_bias,
):
    frames_dev, tiles_dev, side_len, _ = video_in.shape
    channels = norm1_gain.shape[0]
    voxels = video_in.reshape(frames_dev, tiles_dev, side_len, side_len, channels)
    first_frame = lax.axis_index("tm") * frames_dev
    home_ids = lax.axis_index("space") * tiles_dev + jnp.arange(tiles_dev, dtype=jnp.int32)
    home_valid = jnp.take(valid_frames, home_ids)
    nearby = jnp.take(neighbours, home_ids, axis=0)
    frame_pos = first_frame + jnp.arange(frames_dev, dtype=jnp.int32)
    present = (frame_pos[:, None] < home_valid[None, :]).astype(jnp.bfloat16)
    masked = voxels * present[:, :, None, None, None]
    activation = norm_silu(masked.astype(jnp.float32), norm1_gain).astype(jnp.bfloat16)

    def frame_weights(tile_valid):
        return (frame_pos < tile_valid).astype(jnp.float32)[:, None, None, None]

    def first_worker(pieces, tile_valid):
        summed = conv_tile(pieces[0], conv1_weight)
        return norm_silu((summed + conv1_bias) * frame_weights(tile_valid), norm2_gain).astype(
            jnp.bfloat16
        )

    def second_worker(pieces, tile_valid):
        summed = conv_tile(pieces[0], conv2_weight)
        return (
            (summed + conv2_bias) * frame_weights(tile_valid) + pieces[1].astype(jnp.float32)
        ).astype(jnp.bfloat16)

    padded = extend(activation, nearby)
    hidden = home_tiles((padded,), home_valid, first_frame, first_worker)
    padded = extend(hidden, nearby)
    block_out = home_tiles((padded, masked), home_valid, first_frame, second_worker)
    return block_out.reshape(frames_dev, tiles_dev, side_len, side_len * channels)


LANE = 256


def normed(v, half_gain, mask):
    square = jnp.mean(v * v, axis=-1, keepdims=True)
    u = v * (lax.rsqrt(square + epsilon) * mask) * half_gain
    return u + u * jnp.tanh(u)


def put(buf, x, f0, h):
    n, side, channels = h.shape
    row = lax.broadcasted_iota(jnp.int32, h.shape, 1)
    down = jnp.where(row == 0, 0.0, pltpu.roll(h, 1, 1))
    up = jnp.where(row == side - 1, 0.0, pltpu.roll(h, side - 1, 1))
    zero = jnp.zeros((n, side, LANE - channels), jnp.bfloat16)
    for q, t in enumerate((down, h, up)):
        buf[x, f0 : f0 + n, :, q * LANE : q * LANE + channels] = t.astype(jnp.bfloat16)
        buf[x, f0 : f0 + n, :, q * LANE + channels : (q + 1) * LANE] = zero


def spread_one(flat, weight, p, q):
    channels = weight.shape[2]
    zero = jnp.zeros((LANE - channels, channels), weight.dtype)
    turned = flat[3 * p + q].T
    for r in range(3):
        weight[p * 3 + r, q * LANE : q * LANE + channels] = turned[r * channels : (r + 1) * channels]
        weight[p * 3 + r, q * LANE + channels : (q + 1) * LANE] = zero


def spreads(flat, weight):
    return [partial(spread_one, flat, weight, p, q) for p in range(3) for q in range(3)]


def conv(buf, starts, width, f0, frames, weight, accs, beside=()):
    side, channels = buf.shape[2], weight.shape[2]
    totals = [None] * len(starts)
    done = 0
    for tap in range(9):
        p, r = divmod(tap, 3)
        for k, x0 in enumerate(starts):
            rows = buf[x0 + r : x0 + r + width, f0 + p : f0 + p + frames].reshape(-1, 3 * LANE)
            term = jnp.dot(rows, weight[tap], preferred_element_type=jnp.float32)
            totals[k] = term if totals[k] is None else totals[k] + term
        while done * 9 < len(beside) * (tap + 1):
            beside[done]()
            done += 1
    views = []
    for total, acc in zip(totals, accs):
        acc[0:width, 0:frames] = total.reshape(width, frames, side, channels)
        views += [acc.at[g, 0:frames] for g in range(width)]
    return views


def there(f0, frames, valid):
    frame = f0 + lax.broadcasted_iota(jnp.int32, (frames, 1, 1), 0)
    return ((frame >= 0) & (frame < valid)).astype(jnp.float32)


def act(buf, pair, mask, x, at, gain):
    channels = gain.shape[1]
    values = pair.astype(jnp.float32)
    for j in range(2):
        put(buf, x + j, at, normed(values[:, :, j * channels : (j + 1) * channels], gain, mask))


def acts(buf, tile, mask, at, gain):
    lanes = 2 * gain.shape[1]

    def one(k):
        act(buf, tile[:, :, k * lanes : (k + 1) * lanes], mask, 2 + 2 * k, at, gain)

    return [partial(one, k) for k in range(tile.shape[2] // lanes)]


def row_of(ref):
    return ref[...].reshape(1, -1)


def hides(totals, buf, places, at, bias, gain, masks):
    def one(g):
        total = totals[g][...]
        put(buf, places[g], at, normed(total + bias, gain, masks[g]))

    return [partial(one, g) for g in range(len(places))]


def ended(totals, own, lanes, bias, mask):
    parts = [total[...] + bias for total in totals]
    both = jnp.concatenate([part * mask for part in parts], axis=-1)
    return (both + own[:, :, lanes].astype(jnp.float32) * mask).astype(jnp.bfloat16)


def finishes(totals, out, own, x0, at, bias, mask):
    channels = bias.shape[1]

    def one(g):
        lanes = pl.ds((x0 + g) * channels, 2 * channels)
        out[:, :, pl.ds((at + g) * channels, 2 * channels)] = ended(totals[g : g + 2], own, lanes, bias, mask)

    return [partial(one, g) for g in range(0, len(totals), 2)]


def run(works):
    for work in works:
        work()


def load_kernel(far, own, mine, sem):
    lanes = mine.shape[3]
    copies = [
        pltpu.make_async_copy(far.at[:, :, pl.ds(0, lanes)], mine.at[0], sem.at[0]),
        pltpu.make_async_copy(far.at[:, :, pl.ds(far.shape[2] - lanes, lanes)], mine.at[1], sem.at[1]),
        pltpu.make_async_copy(far, own, sem.at[2]),
    ]
    for copy in copies:
        copy.start()
    for copy in copies:
        copy.wait()


def tile_kernel(nb, vf, own, gain1, far1, far2, buf1, mask, flat1, flat2, beside, sem):
    frames = own.shape[0]
    copies = [pltpu.make_async_copy(far1, flat1, sem.at[0]), pltpu.make_async_copy(far2, flat2, sem.at[1])]
    for copy in copies:
        copy.start()
    for tile in range(nb.shape[0]):
        beside[2 * tile] = nb[tile, LEFT]
        beside[2 * tile + 1] = nb[tile, RIGHT]
    first, valid = lax.axis_index("tm") * frames, tracks(nb, vf)[0]
    frame = first - frames + lax.broadcasted_iota(jnp.int32, mask.shape, 0)
    mask[...] = ((frame >= 0) & (frame < valid)).astype(jnp.float32)
    run(acts(buf1, own, there(first, frames, valid), frames, 0.5 * row_of(gain1)))
    for copy in copies:
        copy.wait()


def late_kernel(mask, buf1, flat1, flat2, bias1, gain2, nb, weight1, weight2, buf2, flag, acc):
    k = lax.broadcasted_iota(jnp.int32, nb.shape, 1)
    beyond = jnp.where((k < LEFT) | (k > RIGHT), nb.shape[0] - nb[...], 0)
    flag[0] = jnp.max(beyond)
    frames = buf1.shape[1] // 2
    inner = buf2.shape[0] - 4
    run(spreads(flat1, weight1))
    works = spreads(flat2, weight2)
    totals = conv(buf1, (2,), inner, frames, frames - 2, weight1, (acc,), works)
    masks = [mask[frames + 2 :, :, :1]] * inner
    run(hides(totals, buf2, range(2, 2 + inner), 4, row_of(bias1), 0.5 * row_of(gain2), masks))


def split_of(columns):
    half = (columns - 4) // 2
    return half, half + 2, columns - 4 - half


def early_kernel(mask, prev, gain1, weight1, old1, buf1, acc):
    frames = prev.shape[0]
    _, wide, _ = split_of(prev.shape[2] // gain1.shape[0])
    before = acts(buf1, prev, mask[:frames, :, :1], 0, 0.5 * row_of(gain1))
    needed = (wide + 3) // 2
    run(before[:needed])
    conv(buf1, (2,), wide, frames - 4, 4, weight1, (acc,), before[needed:])


def main_kernel(mask, own, buf1, acc, weight1, bias1, gain2, weight2, bias2, old2, buf2, out, *accs):
    frames = own.shape[0]
    columns = buf2.shape[0] - 2
    half, wide, rest = split_of(columns)
    norm = (0, row_of(bias1), 0.5 * row_of(gain2), [mask[frames - 2 : frames + 2, :, :1]] * columns)
    present = mask[frames:, :, :1]
    works = hides([acc.at[g] for g in range(wide)], buf2, range(2, 2 + wide), *norm)
    totals = conv(buf1, (2 + wide,), rest, frames - 4, 4, weight1, accs[0:1], works)
    works = hides(totals, buf2, range(2 + wide, columns), *norm)
    totals = conv(buf2, (2,), half, 0, frames, weight2, accs[1:2], works)
    works = finishes(totals, out, own, 2, 0, row_of(bias2), present)
    totals = conv(buf2, (2 + half,), rest, 0, frames, weight2, accs[2:3], works)
    run(finishes(totals, out, own, 2 + half, half, row_of(bias2), present))


def rim_kernel(nb, vf, own, rim, prev_rim, gain1, weight1, bias1, gain2, weight2, bias2, old1, old2, inner, buf1, buf2, out, *scratch):
    *accs, staged, sem = scratch
    frames, _, merged = own.shape
    columns = buf2.shape[0] - 2
    first = lax.axis_index("tm") * frames
    valid, left, right = tracks(nb, vf)
    ends = staged.shape[3]
    copies = [pltpu.make_async_copy(inner, out.at[:, :, pl.ds(ends, merged - 2 * ends)], sem.at[2])]
    copies[0].start()
    for side, (x, v) in enumerate(((0, left), (columns + 2, right))):
        act(buf1, prev_rim[side], there(first - frames, frames, v), x, 0, 0.5 * row_of(gain1))
        act(buf1, rim[side], there(first, frames, v), x, frames, 0.5 * row_of(gain1))
    totals = conv(buf1, (0, columns), 2, frames - 4, frames + 2, weight1, accs[0:2])
    places = (0, 1, columns, columns + 1)
    masks = [there(first - 2, frames + 2, v) for v in (left, valid, valid, right)]
    run(hides(totals, buf2, places, 0, row_of(bias1), 0.5 * row_of(gain2), masks))
    totals = conv(buf2, (0, columns - 2), 2, 0, frames, weight2, accs[2:4])
    for side, lane in enumerate((0, merged - ends)):
        lanes = pl.ds(lane, ends)
        staged[side] = ended(totals[2 * side : 2 * side + 2], own, lanes, row_of(bias2), there(first, frames, valid))
        copies.append(pltpu.make_async_copy(staged.at[side], out.at[:, :, lanes], sem.at[side]))
        copies[-1].start()
    for copy in copies:
        copy.wait()


LEFT, RIGHT = 3, 4


def tracks(nb, vf):
    me = lax.axis_index("space")
    tiles = nb.shape[0]

    def of(tile):
        return jnp.where(tile < tiles, vf[jnp.minimum(tile, tiles - 1)], 0)

    return vf[me], of(nb[me, LEFT]), of(nb[me, RIGHT])


def pick_kernel(beside, mine, pair, *outs):
    tiles = beside.shape[0] // 2
    me = lax.axis_index("space")
    for step, out in enumerate(outs):
        there = lax.rem(me + 2 * (step + 1), tiles)
        for side in range(2):
            source = beside[2 * there + side]

            @pl.when(source == me)
            def _():
                out[side] = mine[1 - side]

            @pl.when(source != me)
            def _():
                out[side] = pair[1 - side]


def rims_kernel(beside, mine, pair, *rest):
    received, out = rest[:-1], rest[-1]
    tiles = beside.shape[0] // 2
    half = tiles // 2
    me = lax.axis_index("space")
    for side in range(2):
        source = beside[2 * me + side]
        step = lax.rem(me // 2 - source // 2 + tiles, half)
        at_home = (step == 0) | (source >= tiles)

        @pl.when(at_home & (source == me ^ 1))
        def _():
            out[side] = pair[1 - side]

        @pl.when(at_home & (source != me ^ 1))
        def _():
            out[side] = mine[1 - side]

        for s, arrived in enumerate(received):

            @pl.when((step == s + 1) & (source < tiles))
            def _():
                out[side] = arrived[side]


def exchange(own, mine, beside):
    count = lax.axis_size("space")
    vmem = pl.BlockSpec(memory_space=pltpu.VMEM)
    smem = pl.BlockSpec(memory_space=pltpu.SMEM)
    pair = lax.ppermute(mine, "space", [(i, i ^ 1) for i in range(count)])
    piece = jax.ShapeDtypeStruct(mine.shape, mine.dtype)
    steps = count // 2 - 1
    sent = pl.pallas_call(
        pick_kernel,
        out_shape=[piece] * steps,
        in_specs=[smem, vmem, vmem],
        out_specs=[vmem] * steps,
        compiler_params=pltpu.CompilerParams(vmem_limit_bytes=8 * 2**20),
    )(beside, mine, pair)
    received = []
    for s, value in enumerate(sent):
        received.append(lax.ppermute(value, "space", [(i, (i + 2 * (s + 1)) % count) for i in range(count)]))
    prev = shifted(own, "tm", 1)
    rim = pl.pallas_call(
        rims_kernel,
        out_shape=piece,
        in_specs=[smem] + [vmem] * (2 + steps),
        out_specs=vmem,
        compiler_params=pltpu.CompilerParams(vmem_limit_bytes=8 * 2**20),
    )(beside, mine, pair, *received)
    return prev, rim


def call(kernel, cost, outs, ins, args, places=None, **more):
    flops, moved = cost
    return pl.pallas_call(
        kernel,
        out_shape=outs,
        in_specs=ins,
        out_specs=[VM] * len(outs) if places is None else places,
        cost_estimate=pl.CostEstimate(flops=flops, bytes_accessed=moved, transcendentals=0),
        compiler_params=pltpu.CompilerParams(vmem_limit_bytes=24 * 2**20),
        **more,
    )(*args)


VM = pl.BlockSpec(memory_space=pltpu.VMEM)
SM = pl.BlockSpec(memory_space=pltpu.SMEM)
HB = pl.BlockSpec(memory_space=pl.ANY)


def rooms(side, channels):
    def room(width, frames):
        return pltpu.VMEM((width, frames, side, channels), jnp.float32)

    return room


def row_path(video_in, neighbours, valid_frames, gain1, weight1, bias1, gain2, weight2, bias2):
    far = video_in[:, 0]
    frames, side, merged = far.shape
    channels = gain1.shape[0]
    columns = merged // channels
    tables = (neighbours, valid_frames)
    room = rooms(side, channels)
    one = 2 * 27 * channels * channels * side
    flat = pltpu.VMEM((9, channels, 3 * channels), jnp.bfloat16)
    own, mine = call(
        load_kernel,
        (one, far.size),
        [pltpu.VMEM(far.shape, far.dtype), pltpu.VMEM((2, frames, side, 2 * channels), far.dtype)],
        [HB],
        (far,),
        scratch_shapes=[pltpu.SemaphoreType.DMA((3,))],
    )
    space1 = pltpu.VMEM((columns + 4, 2 * frames, side, 3 * LANE), jnp.bfloat16)
    space2 = pltpu.VMEM((columns + 2, frames + 2, side, 3 * LANE), jnp.bfloat16)
    spaced = pltpu.VMEM((9, 3 * LANE, channels), jnp.bfloat16)
    buf1, mask, flat1, flat2, beside = call(
        tile_kernel,
        (one * 2 * columns, own.size),
        [space1, pltpu.VMEM((2 * frames, side, 128), jnp.float32), flat, flat, pltpu.SMEM((2 * neighbours.shape[0],), jnp.int32)],
        [SM, SM, VM, VM, HB, HB],
        (*tables, own, gain1, jnp.swapaxes(weight1, 1, 2), jnp.swapaxes(weight2, 1, 2)),
        places=[VM] * 4 + [SM],
        scratch_shapes=[pltpu.SemaphoreType.DMA((2,))],
    )
    prev, rim = exchange(far, mine, beside)
    prev_rim = shifted(rim, "tm", 1)
    wide1, wide2, buf2, flag = call(
        late_kernel,
        (one * 4 * columns, own.size),
        [spaced, spaced, space2, pltpu.SMEM((1,), jnp.int32)],
        [VM] * 7,
        (mask, buf1, flat1, flat2, bias1, gain2, neighbours),
        places=[VM] * 3 + [SM],
        scratch_shapes=[room(columns - 2, frames - 2)],
    )
    buf1, acc = call(
        early_kernel,
        (one * 3 * columns, own.size),
        [space1, room(split_of(columns)[1], 4)],
        [VM] * 5,
        (mask, prev, gain1, wide1, buf1),
        input_output_aliases={4: 0},
    )
    buf2, inner = call(
        main_kernel,
        (one * 8 * columns, own.size),
        [space2, pltpu.VMEM((frames, side, (columns - 4) * channels), own.dtype)],
        [VM] * 10,
        (mask, own, buf1, acc, wide1, bias1, gain2, wide2, bias2, buf2),
        input_output_aliases={9: 0},
        scratch_shapes=[room(columns // 2, 4)] + [room(columns // 2, frames)] * 2,
    )
    return flag, (own, rim, prev_rim, wide1, wide2, buf1, buf2, inner)


def row_end(state, tables, gain1, bias1, gain2, bias2):
    own, rim, prev_rim, wide1, wide2, buf1, buf2, inner = state
    space1, space2 = pltpu.VMEM(buf1.shape, buf1.dtype), pltpu.VMEM(buf2.shape, buf2.dtype)
    room = rooms(own.shape[1], gain1.shape[0])
    _, _, out = call(
        rim_kernel,
        (own.size * 1000, own.size),
        [space1, space2, jax.ShapeDtypeStruct(own.shape, own.dtype)],
        [SM, SM] + [VM] * 12,
        (*tables, own, rim, prev_rim, gain1, wide1, bias1, gain2, wide2, bias2, buf1, buf2, inner),
        places=[VM, VM, HB],
        input_output_aliases={11: 0, 12: 1},
        scratch_shapes=[room(2, own.shape[0] + 2)] * 4 + [pltpu.VMEM(rim.shape, rim.dtype), pltpu.SemaphoreType.DMA((3,))],
    )
    return out[:, None]


def on_device(*args):
    video_in, neighbours, _, gain1, _, bias1, gain2, _, bias2 = args
    frames_dev, tiles_dev = video_in.shape[:2]
    tiles = neighbours.shape[0]
    if tiles_dev != 1 or tiles % 2 or frames_dev != 4:
        return general_path(*args)
    flag, state = row_path(*args)
    return lax.cond(
        flag[0] > 0,
        lambda state, args: general_path(*args),
        lambda state, args: row_end(state, args[1:3], gain1, bias1, gain2, bias2),
        state,
        args,
    )


def solution(mesh):
    in_specs = (P("tm", "space", None, None), P(), P(), P(), P(), P(), P(), P(), P())
    out_specs = P("tm", "space", None, None)
    return jax.shard_map(
        on_device, mesh=mesh, in_specs=in_specs, out_specs=out_specs, check_vma=False
    )
```

```python
from functools import partial

import jax
import jax.numpy as jnp
from jax import lax
from jax.experimental import pallas as pl
from jax.experimental.pallas import tpu as pltpu
from jax.sharding import PartitionSpec as P

epsilon = 1e-06


def shifted(value, axis, steps):
    count = lax.axis_size(axis)
    first, last = (max(0, -steps), min(count, count - steps))
    return lax.ppermute(value, axis, [(source, source + steps) for source in range(first, last)])


def norm_silu(values, scale_gain):
    square = jnp.mean(values * values, axis=-1, keepdims=True)
    return jax.nn.silu(values * lax.rsqrt(square + epsilon) * scale_gain)


def conv_tile(framed, weight):
    frames_out = framed.shape[0] - 2
    side_len = framed.shape[1] - 2
    channels = framed.shape[-1]
    widened = jnp.concatenate(
        [framed[:, :, col_off : col_off + side_len] for col_off in range(3)], axis=-1
    )

    def tap(index, summed):
        start = (index // 3, index % 3, 0, 0)
        window = lax.dynamic_slice(widened, start, (frames_out, side_len, side_len, 3 * channels))
        taps = lax.dynamic_index_in_dim(weight, index, 0, keepdims=False)
        return summed + jnp.dot(window.reshape(-1, 3 * channels), taps, preferred_element_type=jnp.float32)

    summed = lax.fori_loop(0, 9, tap, jnp.zeros((frames_out * side_len * side_len, channels), jnp.float32))
    return summed.reshape(frames_out, side_len, side_len, channels)


def edge_pack(activation):
    return jnp.stack(
        [
            activation[:, :, -1],
            activation[:, :, :, -1],
            activation[:, :, :, 0],
            activation[:, :, 0],
        ],
        axis=2,
    )


def fold_edges(totals, portion, offset, nearby):
    amount = portion.shape[1]
    tile_ids = jnp.arange(amount, dtype=jnp.int32)
    choose = (nearby[:, :, None] == tile_ids[None, None, :]).astype(jnp.bfloat16)
    side_choose = jnp.stack([choose[:, 1], choose[:, 3], choose[:, 4], choose[:, 6]], axis=1)
    corner_choose = jnp.stack([choose[:, 0], choose[:, 2], choose[:, 5], choose[:, 7]], axis=1)
    corner_source = jnp.stack(
        [portion[:, :, 0, -1], portion[:, :, 0, 0], portion[:, :, 3, -1], portion[:, :, 3, 0]],
        axis=2,
    )
    new_sides = jnp.einsum(
        "djn,fnjxc->fdjxc", side_choose, portion, preferred_element_type=jnp.float32
    )
    new_corners = jnp.einsum(
        "djn,fnjc->fdjc", corner_choose, corner_source, preferred_element_type=jnp.float32
    )
    return (new_sides.astype(jnp.bfloat16), new_corners.astype(jnp.bfloat16))


def empty_rims(frame_count, activation):
    tiles_dev, side_len, channels = (activation.shape[1], activation.shape[2], activation.shape[4])
    return (
        jnp.zeros((frame_count, tiles_dev, 4, side_len, channels), jnp.bfloat16),
        jnp.zeros((frame_count, tiles_dev, 4, channels), jnp.bfloat16),
    )


def assemble(longer, side_rims, corners):
    top_row = jnp.concatenate([corners[:, :, 0:1], side_rims[:, :, 0], corners[:, :, 1:2]], axis=2)
    bottom_row = jnp.concatenate(
        [corners[:, :, 2:3], side_rims[:, :, 3], corners[:, :, 3:4]], axis=2
    )
    middle = jnp.concatenate(
        [side_rims[:, :, 1][:, :, :, None], longer, side_rims[:, :, 2][:, :, :, None]], axis=3
    )
    return jnp.concatenate([top_row[:, :, None], middle, bottom_row[:, :, None]], axis=2)


def extend(activation, nearby):
    frames_dev = activation.shape[0]
    folder = partial(fold_edges, nearby=nearby)
    side_rims, corners = folder(
        empty_rims(frames_dev, activation),
        lax.all_gather(edge_pack(activation), "space", axis=1, tiled=True),
        jnp.int32(0),
    )
    prev_act, prev_sides, prev_corners = shifted(
        (activation[frames_dev - 2 :], side_rims[frames_dev - 2 :], corners[frames_dev - 2 :]),
        "tm",
        1,
    )
    longer = jnp.concatenate([prev_act, activation], axis=0)
    side_rims = jnp.concatenate([prev_sides, side_rims], axis=0)
    corners = jnp.concatenate([prev_corners, corners], axis=0)
    return assemble(longer, side_rims, corners)


def blank_tile(pieces, tile_valid):
    framed = pieces[0]
    return jnp.zeros(
        (framed.shape[0] - 2, framed.shape[1] - 2, framed.shape[2] - 2, framed.shape[3]),
        jnp.bfloat16,
    )


def home_tiles(inputs, home_valid, first_frame, worker):
    pieces = tuple((stacked[:, 0] for stacked in inputs))
    results = [lax.cond(home_valid[0] > first_frame, worker, blank_tile, pieces, home_valid[0])]
    return jnp.stack(results, axis=1)


def general_path(
    video_in,
    neighbours,
    valid_frames,
    norm1_gain,
    conv1_weight,
    conv1_bias,
    norm2_gain,
    conv2_weight,
    conv2_bias,
):
    frames_dev, tiles_dev, side_len, _ = video_in.shape
    channels = norm1_gain.shape[0]
    voxels = video_in.reshape(frames_dev, tiles_dev, side_len, side_len, channels)
    first_frame = lax.axis_index("tm") * frames_dev
    home_ids = lax.axis_index("space") * tiles_dev + jnp.arange(tiles_dev, dtype=jnp.int32)
    home_valid = jnp.take(valid_frames, home_ids)
    nearby = jnp.take(neighbours, home_ids, axis=0)
    frame_pos = first_frame + jnp.arange(frames_dev, dtype=jnp.int32)
    present = (frame_pos[:, None] < home_valid[None, :]).astype(jnp.bfloat16)
    masked = voxels * present[:, :, None, None, None]
    activation = norm_silu(masked.astype(jnp.float32), norm1_gain).astype(jnp.bfloat16)

    def frame_weights(tile_valid):
        return (frame_pos < tile_valid).astype(jnp.float32)[:, None, None, None]

    def first_worker(pieces, tile_valid):
        summed = conv_tile(pieces[0], conv1_weight)
        return norm_silu((summed + conv1_bias) * frame_weights(tile_valid), norm2_gain).astype(
            jnp.bfloat16
        )

    def second_worker(pieces, tile_valid):
        summed = conv_tile(pieces[0], conv2_weight)
        return (
            (summed + conv2_bias) * frame_weights(tile_valid) + pieces[1].astype(jnp.float32)
        ).astype(jnp.bfloat16)

    padded = extend(activation, nearby)
    hidden = home_tiles((padded,), home_valid, first_frame, first_worker)
    padded = extend(hidden, nearby)
    block_out = home_tiles((padded, masked), home_valid, first_frame, second_worker)
    return block_out.reshape(frames_dev, tiles_dev, side_len, side_len * channels)


LANE = 256


def normed(v, half_gain, mask):
    square = jnp.mean(v * v, axis=-1, keepdims=True)
    u = v * (lax.rsqrt(square + epsilon) * mask) * half_gain
    return u + u * jnp.tanh(u)


def put(buf, x, f0, h):
    n, side, channels = h.shape
    row = lax.broadcasted_iota(jnp.int32, h.shape, 1)
    down = jnp.where(row == 0, 0.0, pltpu.roll(h, 1, 1))
    up = jnp.where(row == side - 1, 0.0, pltpu.roll(h, side - 1, 1))
    zero = jnp.zeros((n, side, LANE - channels), jnp.bfloat16)
    for q, t in enumerate((down, h, up)):
        buf[x, f0 : f0 + n, :, q * LANE : q * LANE + channels] = t.astype(jnp.bfloat16)
        buf[x, f0 : f0 + n, :, q * LANE + channels : (q + 1) * LANE] = zero


def spread_one(flat, weight, p, q):
    channels = weight.shape[2]
    zero = jnp.zeros((LANE - channels, channels), weight.dtype)
    turned = flat[3 * p + q].T
    for r in range(3):
        weight[p * 3 + r, q * LANE : q * LANE + channels] = turned[r * channels : (r + 1) * channels]
        weight[p * 3 + r, q * LANE + channels : (q + 1) * LANE] = zero


def spreads(flat, weight):
    return [partial(spread_one, flat, weight, p, q) for p in range(3) for q in range(3)]


def conv(buf, starts, width, f0, frames, weight, accs, beside=()):
    side, channels = buf.shape[2], weight.shape[2]
    totals = [None] * len(starts)
    done = 0
    for tap in range(9):
        p, r = divmod(tap, 3)
        for k, x0 in enumerate(starts):
            rows = buf[x0 + r : x0 + r + width, f0 + p : f0 + p + frames].reshape(-1, 3 * LANE)
            term = jnp.dot(rows, weight[tap], preferred_element_type=jnp.float32)
            totals[k] = term if totals[k] is None else totals[k] + term
        while done * 9 < len(beside) * (tap + 1):
            beside[done]()
            done += 1
    views = []
    for total, acc in zip(totals, accs):
        acc[0:width, 0:frames] = total.reshape(width, frames, side, channels)
        views += [acc.at[g, 0:frames] for g in range(width)]
    return views


def there(f0, frames, valid):
    frame = f0 + lax.broadcasted_iota(jnp.int32, (frames, 1, 1), 0)
    return ((frame >= 0) & (frame < valid)).astype(jnp.float32)


def act(buf, pair, mask, x, at, gain):
    channels = gain.shape[1]
    values = pair.astype(jnp.float32)
    for j in range(2):
        put(buf, x + j, at, normed(values[:, :, j * channels : (j + 1) * channels], gain, mask))


def acts(buf, tile, mask, at, gain):
    lanes = 2 * gain.shape[1]

    def one(k):
        act(buf, tile[:, :, k * lanes : (k + 1) * lanes], mask, 2 + 2 * k, at, gain)

    return [partial(one, k) for k in range(tile.shape[2] // lanes)]


def row_of(ref):
    return ref[...].reshape(1, -1)


def hides(totals, buf, places, at, bias, gain, masks):
    def one(g):
        total = totals[g][...]
        put(buf, places[g], at, normed(total + bias, gain, masks[g]))

    return [partial(one, g) for g in range(len(places))]


def ended(totals, own, lanes, bias, mask):
    parts = [total[...] + bias for total in totals]
    both = jnp.concatenate([part * mask for part in parts], axis=-1)
    return (both + own[:, :, lanes].astype(jnp.float32) * mask).astype(jnp.bfloat16)


def finishes(totals, out, own, x0, at, bias, mask):
    channels = bias.shape[1]

    def one(g):
        lanes = pl.ds((x0 + g) * channels, 2 * channels)
        out[:, :, pl.ds((at + g) * channels, 2 * channels)] = ended(totals[g : g + 2], own, lanes, bias, mask)

    return [partial(one, g) for g in range(0, len(totals), 2)]


def run(works):
    for work in works:
        work()


def load_kernel(far, own, mine, sem):
    lanes = mine.shape[3]
    copies = [
        pltpu.make_async_copy(far.at[:, :, pl.ds(0, lanes)], mine.at[0], sem.at[0]),
        pltpu.make_async_copy(far.at[:, :, pl.ds(far.shape[2] - lanes, lanes)], mine.at[1], sem.at[1]),
        pltpu.make_async_copy(far, own, sem.at[2]),
    ]
    for copy in copies:
        copy.start()
    for copy in copies:
        copy.wait()


def tile_kernel(nb, vf, own, gain1, far1, far2, buf1, mask, flat1, flat2, beside, sem):
    frames = own.shape[0]
    copies = [pltpu.make_async_copy(far1, flat1, sem.at[0]), pltpu.make_async_copy(far2, flat2, sem.at[1])]
    for copy in copies:
        copy.start()
    for tile in range(nb.shape[0]):
        beside[2 * tile] = nb[tile, LEFT]
        beside[2 * tile + 1] = nb[tile, RIGHT]
    for k, value in enumerate(tracks(nb, vf)):
        beside[2 * nb.shape[0] + k] = value
    first, valid = lax.axis_index("tm") * frames, beside[2 * nb.shape[0]]
    frame = first - frames + lax.broadcasted_iota(jnp.int32, mask.shape, 0)
    mask[...] = ((frame >= 0) & (frame < valid)).astype(jnp.float32)
    run(acts(buf1, own, there(first, frames, valid), frames, 0.5 * row_of(gain1)))
    for copy in copies:
        copy.wait()


def late_kernel(mask, buf1, flat1, flat2, bias1, gain2, nb, weight1, weight2, buf2, flag, acc):
    k = lax.broadcasted_iota(jnp.int32, nb.shape, 1)
    beyond = jnp.where((k < LEFT) | (k > RIGHT), nb.shape[0] - nb[...], 0)
    flag[0] = jnp.max(beyond)
    frames = buf1.shape[1] // 2
    inner = buf2.shape[0] - 4
    run(spreads(flat1, weight1))
    works = spreads(flat2, weight2)
    totals = conv(buf1, (2,), inner, frames, frames - 2, weight1, (acc,), works)
    masks = [mask[frames + 2 :, :, :1]] * inner
    run(hides(totals, buf2, range(2, 2 + inner), 4, row_of(bias1), 0.5 * row_of(gain2), masks))


def split_of(columns):
    half = (columns - 4) // 2
    return half, half + 2, columns - 4 - half


def early_kernel(mask, prev, gain1, weight1, old1, buf1, acc):
    frames = prev.shape[0]
    _, wide, _ = split_of(prev.shape[2] // gain1.shape[0])
    before = acts(buf1, prev, mask[:frames, :, :1], 0, 0.5 * row_of(gain1))
    needed = (wide + 3) // 2
    run(before[:needed])
    conv(buf1, (2,), wide, frames - 4, 4, weight1, (acc,), before[needed:])


def main_kernel(mask, own, buf1, acc, weight1, bias1, gain2, weight2, bias2, old2, buf2, out, *accs):
    frames = own.shape[0]
    columns = buf2.shape[0] - 2
    half, wide, rest = split_of(columns)
    norm = (0, row_of(bias1), 0.5 * row_of(gain2), [mask[frames - 2 : frames + 2, :, :1]] * columns)
    present = mask[frames:, :, :1]
    works = hides([acc.at[g] for g in range(wide)], buf2, range(2, 2 + wide), *norm)
    totals = conv(buf1, (2 + wide,), rest, frames - 4, 4, weight1, accs[0:1], works)
    works = hides(totals, buf2, range(2 + wide, columns), *norm)
    totals = conv(buf2, (2,), half, 0, frames, weight2, accs[1:2], works)
    works = finishes(totals, out, own, 2, 0, row_of(bias2), present)
    totals = conv(buf2, (2 + half,), rest, 0, frames, weight2, accs[2:3], works)
    run(finishes(totals, out, own, 2 + half, half, row_of(bias2), present))


def rim_kernel(beside, own, rim, prev_rim, gain1, weight1, bias1, gain2, weight2, bias2, old1, old2, inner, buf1, buf2, out, *scratch):
    *accs, staged, sem = scratch
    frames, _, merged = own.shape
    columns = buf2.shape[0] - 2
    first = lax.axis_index("tm") * frames
    valid, left, right = (beside[beside.shape[0] - 3 + k] for k in range(3))
    ends = staged.shape[3]
    copies = [pltpu.make_async_copy(inner, out.at[:, :, pl.ds(ends, merged - 2 * ends)], sem.at[2])]
    copies[0].start()
    for side, (x, v) in enumerate(((0, left), (columns + 2, right))):
        act(buf1, prev_rim[side], there(first - frames, frames, v), x, 0, 0.5 * row_of(gain1))
        act(buf1, rim[side], there(first, frames, v), x, frames, 0.5 * row_of(gain1))
    totals = conv(buf1, (0, columns), 2, frames - 4, frames + 2, weight1, accs[0:2])
    places = (0, 1, columns, columns + 1)
    masks = [there(first - 2, frames + 2, v) for v in (left, valid, valid, right)]
    run(hides(totals, buf2, places, 0, row_of(bias1), 0.5 * row_of(gain2), masks))
    totals = conv(buf2, (0, columns - 2), 2, 0, frames, weight2, accs[2:4])
    for side, lane in enumerate((0, merged - ends)):
        lanes = pl.ds(lane, ends)
        staged[side] = ended(totals[2 * side : 2 * side + 2], own, lanes, row_of(bias2), there(first, frames, valid))
        copies.append(pltpu.make_async_copy(staged.at[side], out.at[:, :, lanes], sem.at[side]))
        copies[-1].start()
    for copy in copies:
        copy.wait()


LEFT, RIGHT = 3, 4


def tracks(nb, vf):
    me = lax.axis_index("space")
    tiles = nb.shape[0]

    def of(tile):
        return jnp.where(tile < tiles, vf[jnp.minimum(tile, tiles - 1)], 0)

    return vf[me], of(nb[me, LEFT]), of(nb[me, RIGHT])


def pick_kernel(beside, mine, pair, *outs):
    tiles = (beside.shape[0] - 3) // 2
    me = lax.axis_index("space")
    for step, out in enumerate(outs):
        there = lax.rem(me + 2 * (step + 1), tiles)
        for side in range(2):
            source = beside[2 * there + side]

            @pl.when(source == me)
            def _():
                out[side] = mine[1 - side]

            @pl.when(source != me)
            def _():
                out[side] = pair[1 - side]


def rims_kernel(beside, mine, pair, *rest):
    received, out = rest[:-1], rest[-1]
    tiles = (beside.shape[0] - 3) // 2
    half = tiles // 2
    me = lax.axis_index("space")
    for side in range(2):
        source = beside[2 * me + side]
        step = lax.rem(me // 2 - source // 2 + tiles, half)
        at_home = (step == 0) | (source >= tiles)

        @pl.when(at_home & (source == me ^ 1))
        def _():
            out[side] = pair[1 - side]

        @pl.when(at_home & (source != me ^ 1))
        def _():
            out[side] = mine[1 - side]

        for s, arrived in enumerate(received):

            @pl.when((step == s + 1) & (source < tiles))
            def _():
                out[side] = arrived[side]


def exchange(own, mine, beside):
    count = lax.axis_size("space")
    vmem = pl.BlockSpec(memory_space=pltpu.VMEM)
    smem = pl.BlockSpec(memory_space=pltpu.SMEM)
    pair = lax.ppermute(mine, "space", [(i, i ^ 1) for i in range(count)])
    piece = jax.ShapeDtypeStruct(mine.shape, mine.dtype)
    steps = count // 2 - 1
    sent = pl.pallas_call(
        pick_kernel,
        out_shape=[piece] * steps,
        in_specs=[smem, vmem, vmem],
        out_specs=[vmem] * steps,
        compiler_params=pltpu.CompilerParams(vmem_limit_bytes=8 * 2**20),
    )(beside, mine, pair)
    received = []
    for s, value in enumerate(sent):
        received.append(lax.ppermute(value, "space", [(i, (i + 2 * (s + 1)) % count) for i in range(count)]))
    prev = shifted(own, "tm", 1)
    rim = pl.pallas_call(
        rims_kernel,
        out_shape=piece,
        in_specs=[smem] + [vmem] * (2 + steps),
        out_specs=vmem,
        compiler_params=pltpu.CompilerParams(vmem_limit_bytes=8 * 2**20),
    )(beside, mine, pair, *received)
    return prev, rim


def call(kernel, cost, outs, ins, args, places=None, **more):
    flops, moved = cost
    return pl.pallas_call(
        kernel,
        out_shape=outs,
        in_specs=ins,
        out_specs=[VM] * len(outs) if places is None else places,
        cost_estimate=pl.CostEstimate(flops=flops, bytes_accessed=moved, transcendentals=0),
        compiler_params=pltpu.CompilerParams(vmem_limit_bytes=24 * 2**20),
        **more,
    )(*args)


VM = pl.BlockSpec(memory_space=pltpu.VMEM)
SM = pl.BlockSpec(memory_space=pltpu.SMEM)
HB = pl.BlockSpec(memory_space=pl.ANY)


def rooms(side, channels):
    def room(width, frames):
        return pltpu.VMEM((width, frames, side, channels), jnp.float32)

    return room


def row_path(video_in, neighbours, valid_frames, gain1, weight1, bias1, gain2, weight2, bias2):
    far = video_in[:, 0]
    frames, side, merged = far.shape
    channels = gain1.shape[0]
    columns = merged // channels
    tables = (neighbours, valid_frames)
    room = rooms(side, channels)
    one = 2 * 27 * channels * channels * side
    flat = pltpu.VMEM((9, channels, 3 * channels), jnp.bfloat16)
    own, mine = call(
        load_kernel,
        (one, far.size),
        [pltpu.VMEM(far.shape, far.dtype), pltpu.VMEM((2, frames, side, 2 * channels), far.dtype)],
        [HB],
        (far,),
        scratch_shapes=[pltpu.SemaphoreType.DMA((3,))],
    )
    space1 = pltpu.VMEM((columns + 4, 2 * frames, side, 3 * LANE), jnp.bfloat16)
    space2 = pltpu.VMEM((columns + 2, frames + 2, side, 3 * LANE), jnp.bfloat16)
    spaced = pltpu.VMEM((9, 3 * LANE, channels), jnp.bfloat16)
    buf1, mask, flat1, flat2, beside = call(
        tile_kernel,
        (one * 2 * columns, own.size),
        [space1, pltpu.VMEM((2 * frames, side, 128), jnp.float32), flat, flat, pltpu.SMEM((2 * neighbours.shape[0] + 3,), jnp.int32)],
        [SM, SM, VM, VM, HB, HB],
        (*tables, own, gain1, jnp.swapaxes(weight1, 1, 2), jnp.swapaxes(weight2, 1, 2)),
        places=[VM] * 4 + [SM],
        scratch_shapes=[pltpu.SemaphoreType.DMA((2,))],
    )
    prev, rim = exchange(far, mine, beside)
    prev_rim = shifted(rim, "tm", 1)
    wide1, wide2, buf2, flag = call(
        late_kernel,
        (one * 4 * columns, own.size),
        [spaced, spaced, space2, pltpu.SMEM((1,), jnp.int32)],
        [VM] * 7,
        (mask, buf1, flat1, flat2, bias1, gain2, neighbours),
        places=[VM] * 3 + [SM],
        scratch_shapes=[room(columns - 2, frames - 2)],
    )
    buf1, acc = call(
        early_kernel,
        (one * 3 * columns, own.size),
        [space1, room(split_of(columns)[1], 4)],
        [VM] * 5,
        (mask, prev, gain1, wide1, buf1),
        input_output_aliases={4: 0},
    )
    buf2, inner = call(
        main_kernel,
        (one * 8 * columns, own.size),
        [space2, pltpu.VMEM((frames, side, (columns - 4) * channels), own.dtype)],
        [VM] * 10,
        (mask, own, buf1, acc, wide1, bias1, gain2, wide2, bias2, buf2),
        input_output_aliases={9: 0},
        scratch_shapes=[room(columns // 2, 4)] + [room(columns // 2, frames)] * 2,
    )
    return flag, (beside, own, rim, prev_rim, wide1, wide2, buf1, buf2, inner)


def row_end(state, gain1, bias1, gain2, bias2):
    beside, own, rim, prev_rim, wide1, wide2, buf1, buf2, inner = state
    space1, space2 = pltpu.VMEM(buf1.shape, buf1.dtype), pltpu.VMEM(buf2.shape, buf2.dtype)
    room = rooms(own.shape[1], gain1.shape[0])
    _, _, out = call(
        rim_kernel,
        (own.size * 1000, own.size),
        [space1, space2, jax.ShapeDtypeStruct(own.shape, own.dtype)],
        [SM] + [VM] * 12,
        (beside, own, rim, prev_rim, gain1, wide1, bias1, gain2, wide2, bias2, buf1, buf2, inner),
        places=[VM, VM, HB],
        input_output_aliases={10: 0, 11: 1},
        scratch_shapes=[room(2, own.shape[0] + 2)] * 4 + [pltpu.VMEM(rim.shape, rim.dtype), pltpu.SemaphoreType.DMA((3,))],
    )
    return out[:, None]


def on_device(*args):
    video_in, neighbours, _, gain1, _, bias1, gain2, _, bias2 = args
    frames_dev, tiles_dev = video_in.shape[:2]
    tiles = neighbours.shape[0]
    if tiles_dev != 1 or tiles % 2 or frames_dev != 4:
        return general_path(*args)
    flag, state = row_path(*args)
    return lax.cond(
        flag[0] > 0,
        lambda state, args: general_path(*args),
        lambda state, args: row_end(state, gain1, bias1, gain2, bias2),
        state,
        args,
    )


def solution(mesh):
    in_specs = (P("tm", "space", None, None), P(), P(), P(), P(), P(), P(), P(), P())
    out_specs = P("tm", "space", None, None)
    return jax.shard_map(
        on_device, mesh=mesh, in_specs=in_specs, out_specs=out_specs, check_vma=False
    )
```

```python
from functools import partial

import jax
import jax.numpy as jnp
from jax import lax
from jax.experimental import pallas as pl
from jax.experimental.pallas import tpu as pltpu
from jax.sharding import PartitionSpec as P

epsilon = 1e-06


def shifted(value, axis, steps):
    count = lax.axis_size(axis)
    first, last = (max(0, -steps), min(count, count - steps))
    return lax.ppermute(value, axis, [(source, source + steps) for source in range(first, last)])


def norm_silu(values, scale_gain):
    square = jnp.mean(values * values, axis=-1, keepdims=True)
    return jax.nn.silu(values * lax.rsqrt(square + epsilon) * scale_gain)


def conv_tile(framed, weight):
    frames_out = framed.shape[0] - 2
    side_len = framed.shape[1] - 2
    channels = framed.shape[-1]
    widened = jnp.concatenate(
        [framed[:, :, col_off : col_off + side_len] for col_off in range(3)], axis=-1
    )

    def tap(index, summed):
        start = (index // 3, index % 3, 0, 0)
        window = lax.dynamic_slice(widened, start, (frames_out, side_len, side_len, 3 * channels))
        taps = lax.dynamic_index_in_dim(weight, index, 0, keepdims=False)
        return summed + jnp.dot(window.reshape(-1, 3 * channels), taps, preferred_element_type=jnp.float32)

    summed = lax.fori_loop(0, 9, tap, jnp.zeros((frames_out * side_len * side_len, channels), jnp.float32))
    return summed.reshape(frames_out, side_len, side_len, channels)


def edge_pack(activation):
    return jnp.stack(
        [
            activation[:, :, -1],
            activation[:, :, :, -1],
            activation[:, :, :, 0],
            activation[:, :, 0],
        ],
        axis=2,
    )


def fold_edges(totals, portion, offset, nearby):
    amount = portion.shape[1]
    tile_ids = jnp.arange(amount, dtype=jnp.int32)
    choose = (nearby[:, :, None] == tile_ids[None, None, :]).astype(jnp.bfloat16)
    side_choose = jnp.stack([choose[:, 1], choose[:, 3], choose[:, 4], choose[:, 6]], axis=1)
    corner_choose = jnp.stack([choose[:, 0], choose[:, 2], choose[:, 5], choose[:, 7]], axis=1)
    corner_source = jnp.stack(
        [portion[:, :, 0, -1], portion[:, :, 0, 0], portion[:, :, 3, -1], portion[:, :, 3, 0]],
        axis=2,
    )
    new_sides = jnp.einsum(
        "djn,fnjxc->fdjxc", side_choose, portion, preferred_element_type=jnp.float32
    )
    new_corners = jnp.einsum(
        "djn,fnjc->fdjc", corner_choose, corner_source, preferred_element_type=jnp.float32
    )
    return (new_sides.astype(jnp.bfloat16), new_corners.astype(jnp.bfloat16))


def empty_rims(frame_count, activation):
    tiles_dev, side_len, channels = (activation.shape[1], activation.shape[2], activation.shape[4])
    return (
        jnp.zeros((frame_count, tiles_dev, 4, side_len, channels), jnp.bfloat16),
        jnp.zeros((frame_count, tiles_dev, 4, channels), jnp.bfloat16),
    )


def assemble(longer, side_rims, corners):
    top_row = jnp.concatenate([corners[:, :, 0:1], side_rims[:, :, 0], corners[:, :, 1:2]], axis=2)
    bottom_row = jnp.concatenate(
        [corners[:, :, 2:3], side_rims[:, :, 3], corners[:, :, 3:4]], axis=2
    )
    middle = jnp.concatenate(
        [side_rims[:, :, 1][:, :, :, None], longer, side_rims[:, :, 2][:, :, :, None]], axis=3
    )
    return jnp.concatenate([top_row[:, :, None], middle, bottom_row[:, :, None]], axis=2)


def extend(activation, nearby):
    frames_dev = activation.shape[0]
    folder = partial(fold_edges, nearby=nearby)
    side_rims, corners = folder(
        empty_rims(frames_dev, activation),
        lax.all_gather(edge_pack(activation), "space", axis=1, tiled=True),
        jnp.int32(0),
    )
    prev_act, prev_sides, prev_corners = shifted(
        (activation[frames_dev - 2 :], side_rims[frames_dev - 2 :], corners[frames_dev - 2 :]),
        "tm",
        1,
    )
    longer = jnp.concatenate([prev_act, activation], axis=0)
    side_rims = jnp.concatenate([prev_sides, side_rims], axis=0)
    corners = jnp.concatenate([prev_corners, corners], axis=0)
    return assemble(longer, side_rims, corners)


def blank_tile(pieces, tile_valid):
    framed = pieces[0]
    return jnp.zeros(
        (framed.shape[0] - 2, framed.shape[1] - 2, framed.shape[2] - 2, framed.shape[3]),
        jnp.bfloat16,
    )


def home_tiles(inputs, home_valid, first_frame, worker):
    pieces = tuple((stacked[:, 0] for stacked in inputs))
    results = [lax.cond(home_valid[0] > first_frame, worker, blank_tile, pieces, home_valid[0])]
    return jnp.stack(results, axis=1)


def general_path(
    video_in,
    neighbours,
    valid_frames,
    norm1_gain,
    conv1_weight,
    conv1_bias,
    norm2_gain,
    conv2_weight,
    conv2_bias,
):
    frames_dev, tiles_dev, side_len, _ = video_in.shape
    channels = norm1_gain.shape[0]
    voxels = video_in.reshape(frames_dev, tiles_dev, side_len, side_len, channels)
    first_frame = lax.axis_index("tm") * frames_dev
    home_ids = lax.axis_index("space") * tiles_dev + jnp.arange(tiles_dev, dtype=jnp.int32)
    home_valid = jnp.take(valid_frames, home_ids)
    nearby = jnp.take(neighbours, home_ids, axis=0)
    frame_pos = first_frame + jnp.arange(frames_dev, dtype=jnp.int32)
    present = (frame_pos[:, None] < home_valid[None, :]).astype(jnp.bfloat16)
    masked = voxels * present[:, :, None, None, None]
    activation = norm_silu(masked.astype(jnp.float32), norm1_gain).astype(jnp.bfloat16)

    def frame_weights(tile_valid):
        return (frame_pos < tile_valid).astype(jnp.float32)[:, None, None, None]

    def first_worker(pieces, tile_valid):
        summed = conv_tile(pieces[0], conv1_weight)
        return norm_silu((summed + conv1_bias) * frame_weights(tile_valid), norm2_gain).astype(
            jnp.bfloat16
        )

    def second_worker(pieces, tile_valid):
        summed = conv_tile(pieces[0], conv2_weight)
        return (
            (summed + conv2_bias) * frame_weights(tile_valid) + pieces[1].astype(jnp.float32)
        ).astype(jnp.bfloat16)

    padded = extend(activation, nearby)
    hidden = home_tiles((padded,), home_valid, first_frame, first_worker)
    padded = extend(hidden, nearby)
    block_out = home_tiles((padded, masked), home_valid, first_frame, second_worker)
    return block_out.reshape(frames_dev, tiles_dev, side_len, side_len * channels)


LANE = 256


def normed(v, half_gain, mask):
    square = jnp.mean(v * v, axis=-1, keepdims=True)
    u = v * (lax.rsqrt(square + epsilon) * mask) * half_gain
    return u + u * jnp.tanh(u)


def put(buf, x, f0, h):
    n, side, channels = h.shape
    row = lax.broadcasted_iota(jnp.int32, h.shape, 1)
    down = jnp.where(row == 0, 0.0, pltpu.roll(h, 1, 1))
    up = jnp.where(row == side - 1, 0.0, pltpu.roll(h, side - 1, 1))
    zero = jnp.zeros((n, side, LANE - channels), jnp.bfloat16)
    for q, t in enumerate((down, h, up)):
        buf[x, f0 : f0 + n, :, q * LANE : q * LANE + channels] = t.astype(jnp.bfloat16)
        buf[x, f0 : f0 + n, :, q * LANE + channels : (q + 1) * LANE] = zero


def spread_one(flat, weight, p, q):
    channels = weight.shape[2]
    zero = jnp.zeros((LANE - channels, channels), weight.dtype)
    turned = flat[3 * p + q].T
    for r in range(3):
        weight[p * 3 + r, q * LANE : q * LANE + channels] = turned[r * channels : (r + 1) * channels]
        weight[p * 3 + r, q * LANE + channels : (q + 1) * LANE] = zero


def spreads(flat, weight):
    return [partial(spread_one, flat, weight, p, q) for p in range(3) for q in range(3)]


def conv(buf, starts, width, f0, frames, weight, accs, beside=()):
    side, channels = buf.shape[2], weight.shape[2]
    totals = [None] * len(starts)
    done = 0
    for tap in range(9):
        p, r = divmod(tap, 3)
        for k, x0 in enumerate(starts):
            rows = buf[x0 + r : x0 + r + width, f0 + p : f0 + p + frames].reshape(-1, 3 * LANE)
            term = jnp.dot(rows, weight[tap], preferred_element_type=jnp.float32)
            totals[k] = term if totals[k] is None else totals[k] + term
        while done * 9 < len(beside) * (tap + 1):
            beside[done]()
            done += 1
    views = []
    for total, acc in zip(totals, accs):
        acc[0:width, 0:frames] = total.reshape(width, frames, side, channels)
        views += [acc.at[g, 0:frames] for g in range(width)]
    return views


def there(f0, frames, valid):
    frame = f0 + lax.broadcasted_iota(jnp.int32, (frames, 1, 1), 0)
    return ((frame >= 0) & (frame < valid)).astype(jnp.float32)


def act(buf, pair, mask, x, at, gain):
    channels = gain.shape[1]
    values = pair.astype(jnp.float32)
    for j in range(2):
        put(buf, x + j, at, normed(values[:, :, j * channels : (j + 1) * channels], gain, mask))


def acts(buf, tile, mask, at, gain):
    lanes = 2 * gain.shape[1]

    def one(k):
        act(buf, tile[:, :, k * lanes : (k + 1) * lanes], mask, 2 + 2 * k, at, gain)

    return [partial(one, k) for k in range(tile.shape[2] // lanes)]


def row_of(ref):
    return ref[...].reshape(1, -1)


def hides(totals, buf, places, at, bias, gain, masks):
    def one(g):
        total = totals[g][...]
        put(buf, places[g], at, normed(total + bias, gain, masks[g]))

    return [partial(one, g) for g in range(len(places))]


def ended(totals, own, lanes, bias, mask):
    parts = [total[...] + bias for total in totals]
    both = jnp.concatenate([part * mask for part in parts], axis=-1)
    return (both + own[:, :, lanes].astype(jnp.float32) * mask).astype(jnp.bfloat16)


def finishes(totals, out, own, x0, at, bias, mask):
    channels = bias.shape[1]

    def one(g):
        lanes = pl.ds((x0 + g) * channels, 2 * channels)
        out[:, :, pl.ds((at + g) * channels, 2 * channels)] = ended(totals[g : g + 2], own, lanes, bias, mask)

    return [partial(one, g) for g in range(0, len(totals), 2)]


def run(works):
    for work in works:
        work()


def load_kernel(far, far_nb, far_vf, own, mine, nb, vf, sem):
    lanes = mine.shape[3]
    copies = [
        pltpu.make_async_copy(far.at[:, :, pl.ds(0, lanes)], mine.at[0], sem.at[0]),
        pltpu.make_async_copy(far.at[:, :, pl.ds(far.shape[2] - lanes, lanes)], mine.at[1], sem.at[1]),
        pltpu.make_async_copy(far, own, sem.at[2]),
        pltpu.make_async_copy(far_nb, nb, sem.at[3]),
        pltpu.make_async_copy(far_vf, vf, sem.at[4]),
    ]
    for copy in copies:
        copy.start()
    for copy in copies:
        copy.wait()


def tile_kernel(nb, vf, own, gain1, far1, far2, buf1, mask, flat1, flat2, beside, sem):
    frames = own.shape[0]
    copies = [pltpu.make_async_copy(far1, flat1, sem.at[0]), pltpu.make_async_copy(far2, flat2, sem.at[1])]
    for copy in copies:
        copy.start()
    for tile in range(nb.shape[0]):
        beside[2 * tile] = nb[tile, LEFT]
        beside[2 * tile + 1] = nb[tile, RIGHT]
    for k, value in enumerate(tracks(nb, vf)):
        beside[2 * nb.shape[0] + k] = value
    first, valid = lax.axis_index("tm") * frames, beside[2 * nb.shape[0]]
    frame = first - frames + lax.broadcasted_iota(jnp.int32, mask.shape, 0)
    mask[...] = ((frame >= 0) & (frame < valid)).astype(jnp.float32)
    run(acts(buf1, own, there(first, frames, valid), frames, 0.5 * row_of(gain1)))
    for copy in copies:
        copy.wait()


def late_kernel(mask, buf1, flat1, flat2, bias1, gain2, nb, weight1, weight2, buf2, flag, acc):
    k = lax.broadcasted_iota(jnp.int32, nb.shape, 1)
    beyond = jnp.where((k < LEFT) | (k > RIGHT), nb.shape[0] - nb[...], 0)
    flag[0] = jnp.max(beyond)
    frames = buf1.shape[1] // 2
    inner = buf2.shape[0] - 4
    run(spreads(flat1, weight1))
    works = spreads(flat2, weight2)
    totals = conv(buf1, (2,), inner, frames, frames - 2, weight1, (acc,), works)
    masks = [mask[frames + 2 :, :, :1]] * inner
    run(hides(totals, buf2, range(2, 2 + inner), 4, row_of(bias1), 0.5 * row_of(gain2), masks))


def split_of(columns):
    half = (columns - 4) // 2
    return half, half + 2, columns - 4 - half


def early_kernel(mask, prev, gain1, weight1, old1, buf1, acc):
    frames = prev.shape[0]
    _, wide, _ = split_of(prev.shape[2] // gain1.shape[0])
    before = acts(buf1, prev, mask[:frames, :, :1], 0, 0.5 * row_of(gain1))
    needed = (wide + 3) // 2
    run(before[:needed])
    conv(buf1, (2,), wide, frames - 4, 4, weight1, (acc,), before[needed:])


def main_kernel(mask, own, buf1, acc, weight1, bias1, gain2, weight2, bias2, old2, buf2, out, *accs):
    frames = own.shape[0]
    columns = buf2.shape[0] - 2
    half, wide, rest = split_of(columns)
    norm = (0, row_of(bias1), 0.5 * row_of(gain2), [mask[frames - 2 : frames + 2, :, :1]] * columns)
    present = mask[frames:, :, :1]
    works = hides([acc.at[g] for g in range(wide)], buf2, range(2, 2 + wide), *norm)
    totals = conv(buf1, (2 + wide,), rest, frames - 4, 4, weight1, accs[0:1], works)
    works = hides(totals, buf2, range(2 + wide, columns), *norm)
    totals = conv(buf2, (2,), half, 0, frames, weight2, accs[1:2], works)
    works = finishes(totals, out, own, 2, 0, row_of(bias2), present)
    totals = conv(buf2, (2 + half,), rest, 0, frames, weight2, accs[2:3], works)
    run(finishes(totals, out, own, 2 + half, half, row_of(bias2), present))


def rim_kernel(beside, own, rim, prev_rim, gain1, weight1, bias1, gain2, weight2, bias2, old1, old2, inner, buf1, buf2, out, *scratch):
    *accs, staged, sem = scratch
    frames, _, merged = own.shape
    columns = buf2.shape[0] - 2
    first = lax.axis_index("tm") * frames
    valid, left, right = (beside[beside.shape[0] - 3 + k] for k in range(3))
    ends = staged.shape[3]
    copies = [pltpu.make_async_copy(inner, out.at[:, :, pl.ds(ends, merged - 2 * ends)], sem.at[2])]
    copies[0].start()
    for side, (x, v) in enumerate(((0, left), (columns + 2, right))):
        act(buf1, prev_rim[side], there(first - frames, frames, v), x, 0, 0.5 * row_of(gain1))
        act(buf1, rim[side], there(first, frames, v), x, frames, 0.5 * row_of(gain1))
    totals = conv(buf1, (0, columns), 2, frames - 4, frames + 2, weight1, accs[0:2])
    places = (0, 1, columns, columns + 1)
    masks = [there(first - 2, frames + 2, v) for v in (left, valid, valid, right)]
    run(hides(totals, buf2, places, 0, row_of(bias1), 0.5 * row_of(gain2), masks))
    totals = conv(buf2, (0, columns - 2), 2, 0, frames, weight2, accs[2:4])
    for side, lane in enumerate((0, merged - ends)):
        lanes = pl.ds(lane, ends)
        staged[side] = ended(totals[2 * side : 2 * side + 2], own, lanes, row_of(bias2), there(first, frames, valid))
        copies.append(pltpu.make_async_copy(staged.at[side], out.at[:, :, lanes], sem.at[side]))
        copies[-1].start()
    for copy in copies:
        copy.wait()


LEFT, RIGHT = 3, 4


def tracks(nb, vf):
    me = lax.axis_index("space")
    tiles = nb.shape[0]

    def of(tile):
        return jnp.where(tile < tiles, vf[jnp.minimum(tile, tiles - 1)], 0)

    return vf[me], of(nb[me, LEFT]), of(nb[me, RIGHT])


def pick_kernel(beside, mine, pair, *outs):
    tiles = (beside.shape[0] - 3) // 2
    me = lax.axis_index("space")
    for step, out in enumerate(outs):
        there = lax.rem(me + 2 * (step + 1), tiles)
        for side in range(2):
            source = beside[2 * there + side]

            @pl.when(source == me)
            def _():
                out[side] = mine[1 - side]

            @pl.when(source != me)
            def _():
                out[side] = pair[1 - side]


def rims_kernel(beside, mine, pair, *rest):
    received, out = rest[:-1], rest[-1]
    tiles = (beside.shape[0] - 3) // 2
    half = tiles // 2
    me = lax.axis_index("space")
    for side in range(2):
        source = beside[2 * me + side]
        step = lax.rem(me // 2 - source // 2 + tiles, half)
        at_home = (step == 0) | (source >= tiles)

        @pl.when(at_home & (source == me ^ 1))
        def _():
            out[side] = pair[1 - side]

        @pl.when(at_home & (source != me ^ 1))
        def _():
            out[side] = mine[1 - side]

        for s, arrived in enumerate(received):

            @pl.when((step == s + 1) & (source < tiles))
            def _():
                out[side] = arrived[side]


def exchange(own, mine, beside):
    count = lax.axis_size("space")
    vmem = pl.BlockSpec(memory_space=pltpu.VMEM)
    smem = pl.BlockSpec(memory_space=pltpu.SMEM)
    pair = lax.ppermute(mine, "space", [(i, i ^ 1) for i in range(count)])
    piece = jax.ShapeDtypeStruct(mine.shape, mine.dtype)
    steps = count // 2 - 1
    sent = pl.pallas_call(
        pick_kernel,
        out_shape=[piece] * steps,
        in_specs=[smem, vmem, vmem],
        out_specs=[vmem] * steps,
        compiler_params=pltpu.CompilerParams(vmem_limit_bytes=8 * 2**20),
    )(beside, mine, pair)
    received = []
    for s, value in enumerate(sent):
        received.append(lax.ppermute(value, "space", [(i, (i + 2 * (s + 1)) % count) for i in range(count)]))
    prev = shifted(own, "tm", 1)
    rim = pl.pallas_call(
        rims_kernel,
        out_shape=piece,
        in_specs=[smem] + [vmem] * (2 + steps),
        out_specs=vmem,
        compiler_params=pltpu.CompilerParams(vmem_limit_bytes=8 * 2**20),
    )(beside, mine, pair, *received)
    return prev, rim


def call(kernel, cost, outs, ins, args, places=None, **more):
    flops, moved = cost
    return pl.pallas_call(
        kernel,
        out_shape=outs,
        in_specs=ins,
        out_specs=[VM] * len(outs) if places is None else places,
        cost_estimate=pl.CostEstimate(flops=flops, bytes_accessed=moved, transcendentals=0),
        compiler_params=pltpu.CompilerParams(vmem_limit_bytes=24 * 2**20),
        **more,
    )(*args)


VM = pl.BlockSpec(memory_space=pltpu.VMEM)
SM = pl.BlockSpec(memory_space=pltpu.SMEM)
HB = pl.BlockSpec(memory_space=pl.ANY)


def rooms(side, channels):
    def room(width, frames):
        return pltpu.VMEM((width, frames, side, channels), jnp.float32)

    return room


def row_path(video_in, neighbours, valid_frames, gain1, weight1, bias1, gain2, weight2, bias2):
    far = video_in[:, 0]
    frames, side, merged = far.shape
    channels = gain1.shape[0]
    columns = merged // channels
    tables = (neighbours, valid_frames)
    room = rooms(side, channels)
    one = 2 * 27 * channels * channels * side
    flat = pltpu.VMEM((9, channels, 3 * channels), jnp.bfloat16)
    own, mine, *near = call(
        load_kernel,
        (one, far.size),
        [pltpu.VMEM(far.shape, far.dtype), pltpu.VMEM((2, frames, side, 2 * channels), far.dtype)]
        + [pltpu.SMEM(table.shape, table.dtype) for table in tables],
        [HB] * 3,
        (far, *tables),
        places=[VM, VM, SM, SM],
        scratch_shapes=[pltpu.SemaphoreType.DMA((5,))],
    )
    space1 = pltpu.VMEM((columns + 4, 2 * frames, side, 3 * LANE), jnp.bfloat16)
    space2 = pltpu.VMEM((columns + 2, frames + 2, side, 3 * LANE), jnp.bfloat16)
    spaced = pltpu.VMEM((9, 3 * LANE, channels), jnp.bfloat16)
    buf1, mask, flat1, flat2, beside = call(
        tile_kernel,
        (one * 2 * columns, own.size),
        [space1, pltpu.VMEM((2 * frames, side, 128), jnp.float32), flat, flat, pltpu.SMEM((2 * neighbours.shape[0] + 3,), jnp.int32)],
        [SM, SM, VM, VM, HB, HB],
        (*near, own, gain1, jnp.swapaxes(weight1, 1, 2), jnp.swapaxes(weight2, 1, 2)),
        places=[VM] * 4 + [SM],
        scratch_shapes=[pltpu.SemaphoreType.DMA((2,))],
    )
    prev, rim = exchange(far, mine, beside)
    prev_rim = shifted(rim, "tm", 1)
    wide1, wide2, buf2, flag = call(
        late_kernel,
        (one * 4 * columns, own.size),
        [spaced, spaced, space2, pltpu.SMEM((1,), jnp.int32)],
        [VM] * 7,
        (mask, buf1, flat1, flat2, bias1, gain2, neighbours),
        places=[VM] * 3 + [SM],
        scratch_shapes=[room(columns - 2, frames - 2)],
    )
    buf1, acc = call(
        early_kernel,
        (one * 3 * columns, own.size),
        [space1, room(split_of(columns)[1], 4)],
        [VM] * 5,
        (mask, prev, gain1, wide1, buf1),
        input_output_aliases={4: 0},
    )
    buf2, inner = call(
        main_kernel,
        (one * 8 * columns, own.size),
        [space2, pltpu.VMEM((frames, side, (columns - 4) * channels), own.dtype)],
        [VM] * 10,
        (mask, own, buf1, acc, wide1, bias1, gain2, wide2, bias2, buf2),
        input_output_aliases={9: 0},
        scratch_shapes=[room(columns // 2, 4)] + [room(columns // 2, frames)] * 2,
    )
    return flag, (beside, own, rim, prev_rim, wide1, wide2, buf1, buf2, inner)


def row_end(state, gain1, bias1, gain2, bias2):
    beside, own, rim, prev_rim, wide1, wide2, buf1, buf2, inner = state
    space1, space2 = pltpu.VMEM(buf1.shape, buf1.dtype), pltpu.VMEM(buf2.shape, buf2.dtype)
    room = rooms(own.shape[1], gain1.shape[0])
    _, _, out = call(
        rim_kernel,
        (own.size * 1000, own.size),
        [space1, space2, jax.ShapeDtypeStruct(own.shape, own.dtype)],
        [SM] + [VM] * 12,
        (beside, own, rim, prev_rim, gain1, wide1, bias1, gain2, wide2, bias2, buf1, buf2, inner),
        places=[VM, VM, HB],
        input_output_aliases={10: 0, 11: 1},
        scratch_shapes=[room(2, own.shape[0] + 2)] * 4 + [pltpu.VMEM(rim.shape, rim.dtype), pltpu.SemaphoreType.DMA((3,))],
    )
    return out[:, None]


def on_device(*args):
    video_in, neighbours, _, gain1, _, bias1, gain2, _, bias2 = args
    frames_dev, tiles_dev = video_in.shape[:2]
    tiles = neighbours.shape[0]
    if tiles_dev != 1 or tiles % 2 or frames_dev != 4:
        return general_path(*args)
    flag, state = row_path(*args)
    return lax.cond(
        flag[0] > 0,
        lambda state, args: general_path(*args),
        lambda state, args: row_end(state, gain1, bias1, gain2, bias2),
        state,
        args,
    )


def solution(mesh):
    in_specs = (P("tm", "space", None, None), P(), P(), P(), P(), P(), P(), P(), P())
    out_specs = P("tm", "space", None, None)
    return jax.shard_map(
        on_device, mesh=mesh, in_specs=in_specs, out_specs=out_specs, check_vma=False
    )
```
